512 devices in a mesh: chain: 2 (over x_lo), slab: 128 (over x_hi, z, y), vis: 2 (over core).
Axes of the slice: x: 4 (x_hi: 2, x_lo: 2; x = x_hi * 2 + x_lo), y: 8, z: 8, core: 2. Of those that a mesh axis runs over, the one named last changes fastest.
Arguments:
- screens: float32 [4, 2048, 2048], P(('chain', 'vis'), 'slab'), parts along dimension 0, may hold values from -6 to 6
- image: float32 [4096, 2048], P(('chain', 'slab')), parts along dimension 0, may hold values from -6 to 6
- vis_row: int32 [32768], P('slab'), may hold values from 0 to 2047
- vis_block: int32 [32768, 1], P('slab'), may hold values from 0 to 127; in each aligned block of 256 rows (0 to 255, 256 to 511, ...) at most 6 rows name the same one
- vis_column: int32 [32768], P('slab'), may hold values from 0 to 7
- vis_real: float32 [32768], P('slab'), may hold values from -6 to 6
- vis_imag: float32 [32768], P('slab'), may hold values from -6 to 6
- vis_weight: float32 [32768], P('slab'), may hold values from 0.5 to 4
Outputs:
- screen_grad: float32 [4, 2048, 2048], P(('chain', 'vis'), 'slab'), parts along dimension 0
The draws below stay inside these ranges and needn't reach their ends.
There are 2 independent parts, one for each index of `chain`. The reference program is written for one: setup_inputs(seed, part) draws one part's arguments, and reference() takes and returns one part's arrays. A program takes and returns all parts, laid end to end along the dimension named above; an argument that names none is the same for every part. Nothing has to cross between parts.
Inputs may be any that keep to these rules, and one draw needn't show every extreme that they name: `vis_block`: among the 256 visibilities of one index of slab, at most 6 name any one block; in every draw some block of some index holds exactly 6.
All inputs are finite; a program needn't handle non-finite values.
Results may differ from the reference program's by a relative error of at most 0.013.
Values may be sent and summed in bfloat16 or wider, within the bound.
No kernel may reach another device: no remote copies, remote signals or barrier semaphores. Data moves between devices by JAX's collectives and lax.ppermute only.
A program may use at most 64 MiB of HBM per device.

```python
import math
import jax
import jax.numpy as jnp
import numpy as np
from jax import lax

GRID = 2048
VIS_DEV = 256
WALK = 2
VIS = 32768
KX_BLOCK = 8
CAP = 6
N_SLAB = 128


def plant(values, own_key, smallest, largest):
    longest = values.shape.index(max(values.shape))
    spots = []
    for shift in (0, 1):
        where = [jax.random.randint(jax.random.fold_in(own_key, axis), (), 0, length) for axis, length in enumerate(values.shape)]
        where[longest] = (where[longest] + shift) % values.shape[longest]
        spots.append(tuple(where))
    return values.at[spots[0]].set(smallest).at[spots[1]].set(largest)


def block_levels(own_key, extent, cuts, low, top_value):
    gain = 1.0
    for position, parts in cuts:
        draws = jax.random.uniform(jax.random.fold_in(jax.random.fold_in(own_key, 6), position), (parts,), jnp.float32, low / len(cuts), top_value / len(cuts))
        gain = gain * jnp.repeat(jnp.exp(draws), extent[position] // parts).reshape((-1,) + (1,) * (len(extent) - 1 - position))
    return gain


def deal_out(own_key, own, number, rows, amount, top, reach, lean):
    order = jax.random.permutation(own_key, amount)
    heavy_load, ordinary = portions_of(amount, rows * top, reach, lean, True), portions_of(amount, rows * top, reach, lean, False)
    places = jnp.arange(amount)

    def named(sizes, offset_by):
        used = int((sizes > 0).sum())
        fixed = max(1, used // 4)
        passed = fixed + (places - fixed + offset_by * (used - fixed)) % max(1, amount - fixed)
        return jnp.zeros((amount,), jnp.int32).at[order[jnp.where(places < fixed, places, passed)]].set(jnp.asarray(sizes, jnp.int32))

    sizes = jnp.where(number % 4 == 0, named(heavy_load, number // 4), named(ordinary, number - number // 4 - 1))
    mixed = jax.random.permutation(jax.random.fold_in(own, 3), amount)
    giver, sink = mixed[0:amount // 2 * 2:2], mixed[1:amount // 2 * 2:2]
    slack = jnp.minimum(sizes[giver] - 1, reach - sizes[sink]) // 2
    slack = jnp.where((giver == order[0]) | (sink == order[0]) | (sizes[sink] == 0), 0, jnp.maximum(slack, 0))
    passed = jax.random.randint(jax.random.fold_in(own, 4), (amount // 2,), 0, 1 << 20) % (slack + 1)
    sizes = sizes.at[giver].add(-passed).at[sink].add(passed)
    items = jnp.searchsorted(jnp.cumsum(sizes), jnp.arange(rows * top), side="right").astype(jnp.int32)
    table = items.reshape(top, rows).T
    table = table[jax.random.permutation(jax.random.fold_in(own, 1), rows)]
    offset_by = jax.random.randint(jax.random.fold_in(own, 2), (rows, 1), 0, top)
    return jnp.take_along_axis(table, (jnp.arange(top)[None, :] + offset_by) % top, axis=1)


def portions_of(number_of, total, limit, lean, full):
    portions = [(1 << 20) // math.isqrt(standing ** lean) + 1 for standing in range(1, number_of + 1)]
    largest = limit if full else min(limit, max(-(-total // number_of), total * portions[0] // sum(portions)))
    least = 1 if total - largest >= number_of - 1 else 0
    holding, surplus = [largest] + [least] * (number_of - 1), total - largest - least * (number_of - 1)
    while surplus > 0:
        movable = [i for i in range(1, number_of) if holding[i] < largest] or [i for i in range(1, number_of) if holding[i] < limit]
        pool, budget = sum([portions[i] for i in movable]), surplus
        for i in movable:
            extra = min(limit - holding[i], max(1, budget * portions[i] // pool), surplus)
            holding[i] = holding[i] + extra
            surplus = surplus - extra
    return np.array(holding)


def gaussian(rng, shape, width, most, cuts=(), kind=jnp.bfloat16):
    drawn = jax.random.normal(rng, shape, jnp.float32) * width
    if len(cuts) > 0:
        drawn = block_levels(rng, shape, cuts, -0.22, 0.18) * drawn
    return jnp.clip(drawn, min=-most, max=most).astype(kind)


def setup_inputs(seed: int = 0, part: int = 0) -> dict:
    splits = jax.random.split(jax.random.key(seed), 9)
    part_splits = jax.random.split(jax.random.fold_in(splits[8], part), 9)
    screens = gaussian(part_splits[0], (WALK, GRID, GRID), 1.0, 6.0, ((0, 2), (1, 128)), jnp.float32)
    image = gaussian(part_splits[1], (GRID, GRID), 1.0, 6.0, ((0, 128),), jnp.float32)
    vis_row = plant(jax.random.randint(splits[2], (VIS,), 0, GRID), jax.random.fold_in(splits[2], 1), 0, GRID - 1).astype(jnp.int32)
    vis_block_keys = jax.random.split(jax.random.fold_in(splits[3], 1), VIS // VIS_DEV)
    vis_block_turns = jax.random.permutation(jax.random.fold_in(splits[3], 3), VIS // VIS_DEV)
    vis_block = jax.vmap(lambda own, number: deal_out(jax.random.fold_in(splits[3], 2), own, number, VIS_DEV, N_SLAB, 1, CAP, 2))(vis_block_keys, vis_block_turns).reshape((VIS, 1))
    vis_column = plant(jax.random.randint(splits[4], (VIS,), 0, KX_BLOCK), jax.random.fold_in(splits[4], 1), 0, KX_BLOCK - 1).astype(jnp.int32)
    vis_real = gaussian(splits[5], (VIS,), 1.0, 6.0, ((0, 128),), jnp.float32)
    vis_imag = gaussian(splits[6], (VIS,), 1.0, 6.0, ((0, 128),), jnp.float32)
    vis_weight = jnp.clip(jnp.exp(math.log(4.0) - 2.0794415 * jax.random.uniform(splits[7], (VIS,), jnp.float32) ** block_levels(splits[7], (VIS,), ((0, 128),), -0.2, 0.2)), 0.5, 4.0)
    return {"screens": screens, "image": image, "vis_row": vis_row, "vis_block": vis_block, "vis_column": vis_column, "vis_real": vis_real, "vis_imag": vis_imag, "vis_weight": vis_weight}


refract = 1.0

def twiddle(first, second, length):
    phase = (first[:, None] * second[None, :] % length).astype(jnp.float32) * (2.0 * math.pi / length)
    return (jnp.cos(phase).astype(jnp.bfloat16), jnp.sin(phase).astype(jnp.bfloat16))

def col_slope(field):
    return (8.0 * (jnp.roll(field, -1, -1) - jnp.roll(field, 1, -1)) - (jnp.roll(field, -2, -1) - jnp.roll(field, 2, -1))) / 12.0

def col_adjoint(field):
    return (8.0 * (jnp.roll(field, 1, -1) - jnp.roll(field, -1, -1)) - (jnp.roll(field, 2, -1) - jnp.roll(field, -2, -1))) / 12.0

def row_slope(field):
    return (8.0 * (jnp.roll(field, -1, -2) - jnp.roll(field, 1, -2)) - (jnp.roll(field, -2, -2) - jnp.roll(field, 2, -2))) / 12.0

def row_adjoint(field):
    return (8.0 * (jnp.roll(field, 1, -2) - jnp.roll(field, -1, -2)) - (jnp.roll(field, 2, -2) - jnp.roll(field, -2, -2))) / 12.0

def reference(screens, image, vis_row, vis_block, vis_column, vis_real, vis_imag, vis_weight):
    unitary = 1.0 / math.sqrt(GRID)
    half_kx = GRID // 2
    positions = jnp.arange(GRID, dtype=jnp.int32)
    cos_half, sin_half = twiddle(jnp.arange(half_kx, dtype=jnp.int32), positions, GRID)
    image_x = col_slope(image)
    image_y = row_slope(image)
    joined = (image[None] + refract * (col_slope(screens) * image_x[None] + row_slope(screens) * image_y[None])).astype(jnp.bfloat16)
    flat = joined.reshape(WALK * GRID, GRID)
    spec_real = (unitary * jnp.dot(flat, cos_half.T, preferred_element_type=jnp.float32)).astype(jnp.bfloat16)
    spec_imag = (-unitary * jnp.dot(flat, sin_half.T, preferred_element_type=jnp.float32)).astype(jnp.bfloat16)
    trans_real = jnp.transpose(spec_real.reshape(WALK, GRID, half_kx), (0, 2, 1))
    trans_imag = jnp.transpose(spec_imag.reshape(WALK, GRID, half_kx), (0, 2, 1))
    col_index = (vis_block[:, 0] * KX_BLOCK + vis_column).astype(jnp.int32)
    step_size = math.gcd(2048, VIS)
    steps_count = VIS // step_size

    def visit(sums, inputs):
        row_freq, col_freq, real_part, imag_part, weight = inputs
        cos_rows, sin_rows = twiddle(row_freq, positions, GRID)
        cos_full = cos_rows.astype(jnp.float32)[None]
        sin_full = sin_rows.astype(jnp.float32)[None]
        pick_real = trans_real[:, col_freq, :].astype(jnp.float32)
        pick_imag = trans_imag[:, col_freq, :].astype(jnp.float32)
        model_real = unitary * lax.optimization_barrier(jnp.sum(cos_full * pick_real + sin_full * pick_imag, -1))
        model_imag = unitary * lax.optimization_barrier(jnp.sum(cos_full * pick_imag - sin_full * pick_real, -1))
        error_real = lax.optimization_barrier((weight[None] * (model_real - real_part[None])).astype(jnp.bfloat16)).astype(jnp.float32)
        error_imag = lax.optimization_barrier((weight[None] * (model_imag - imag_part[None])).astype(jnp.bfloat16)).astype(jnp.float32)
        term_real = cos_full * error_real[:, :, None] - sin_full * error_imag[:, :, None]
        term_imag = sin_full * error_real[:, :, None] + cos_full * error_imag[:, :, None]
        return ((sums[0].at[:, col_freq, :].add(term_real), sums[1].at[:, col_freq, :].add(term_imag)), None)
    zeros_grid = jnp.zeros((WALK, half_kx, GRID), jnp.float32)
    inputs = (vis_row.astype(jnp.int32).reshape(steps_count, step_size), col_index.reshape(steps_count, step_size), vis_real.reshape(steps_count, step_size), vis_imag.reshape(steps_count, step_size), vis_weight.reshape(steps_count, step_size))
    (sum_real, sum_imag), _ = lax.scan(visit, (zeros_grid, zeros_grid), inputs)
    back_real = (unitary * sum_real).astype(jnp.bfloat16)
    back_imag = (unitary * sum_imag).astype(jnp.bfloat16)
    rows_real = jnp.transpose(back_real, (0, 2, 1)).reshape(WALK * GRID, half_kx)
    rows_imag = jnp.transpose(back_imag, (0, 2, 1)).reshape(WALK * GRID, half_kx)
    gradient = jnp.dot(rows_real, cos_half, preferred_element_type=jnp.float32) - jnp.dot(rows_imag, sin_half, preferred_element_type=jnp.float32)
    gradient = (unitary * gradient).reshape(WALK, GRID, GRID)
    push_x = refract * image_x[None] * gradient
    push_y = refract * image_y[None] * gradient
    return col_adjoint(push_x) + row_adjoint(push_y)
```

```python
import math

import jax
import jax.numpy as jnp
import numpy as np
from jax import lax
from jax.experimental import pallas as pl
from jax.experimental.pallas import tpu as pltpu
from jax.sharding import PartitionSpec as P

F32 = jnp.float32
BF16 = jnp.bfloat16
NT = (((1,), (1,)), ((), ()))
NN = (((1,), (0,)), ((), ()))
fields = 8
halo = 4


def angle(first, second, length):
    turn = (np.outer(first, second) % length) * (2.0 * math.pi / length)
    return np.cos(turn), np.sin(turn)


def tables(rows, slabs, owned, grid):
    fine = grid // slabs
    lanes = owned * rows
    c2, k2, k1 = np.arange(slabs), np.arange(slabs // 2), np.arange(fine)
    cos, sin = angle(k2, c2, slabs)
    row_forward = np.block([[cos, sin], [-sin, cos]])
    row_back = np.block([[cos, sin], [-sin, cos]])
    col_turn = angle(k1, c2, grid)
    cos, sin = angle(c2, c2, slabs)
    coarse = np.block([[cos, sin], [-sin, cos]])
    cos, sin = angle(k1, k1, fine)
    eye = np.eye(owned)
    cos, sin = np.kron(eye, cos), np.kron(eye, sin)
    inner = np.block([[cos, -sin], [sin, cos]])
    row_turn = [np.tile(part, (1, owned)) for part in angle(c2, k1, grid)]
    low = [row_forward, row_back, coarse, coarse.T, inner, inner.T]
    high = [*col_turn, *row_turn]
    assert lanes == slabs
    return [jnp.asarray(t, BF16) for t in low], [jnp.asarray(t, F32) for t in high]


def payload_kernel(row, block, column, real, imag, weight, out, wide):
    vis_count = row.shape[1]
    slabs = out.shape[0]
    hot = (
        lax.broadcasted_iota(jnp.int32, (slabs, vis_count), 0) == block[...]
    ).astype(F32)
    hot_low = hot.astype(BF16)
    earlier = (
        lax.broadcasted_iota(jnp.int32, (vis_count, vis_count), 0)
        < lax.broadcasted_iota(jnp.int32, (vis_count, vis_count), 1)
    ).astype(F32).astype(BF16)
    before = lax.dot_general(hot_low, earlier, NN, preferred_element_type=F32)
    rank = jnp.sum(before * hot, axis=0, keepdims=True)
    ky = row[...]
    parts = [
        jnp.bitwise_and(ky, slabs - 1).astype(F32),
        (column[...] * (slabs // 8) + ky // slabs).astype(F32),
    ]
    for value in (real, imag, weight):
        whole = value[...]
        lead = whole.astype(BF16).astype(F32)
        parts += [lead, whole - lead]
    which = lax.broadcasted_iota(jnp.int32, (fields, vis_count), 0)
    stack = jnp.zeros((fields, vis_count), F32)
    for index, part in enumerate(parts):
        stack = jnp.where(which == index, part, stack)
    for slot in range(slabs // fields):
        wide[slot * fields : (slot + 1) * fields, :] = jnp.where(
            rank == float(slot), stack, 0.0
        )
    out[...] = lax.dot_general(
        hot_low, wide[...].astype(BF16), NT, preferred_element_type=F32
    )


def lane_roll(x, shift):
    return pltpu.roll(x, shift % x.shape[1], 1)


def row_roll(x, shift):
    return pltpu.roll(x, shift % x.shape[0], 0)


def slope(x, roll):
    return (8.0 * (roll(x, -1) - roll(x, 1)) - (roll(x, -2) - roll(x, 2))) * (1.0 / 12.0)


def cosine(index, length):
    return math.cos(2.0 * math.pi * (index % length) / length)


def sine(index, length):
    return math.sin(2.0 * math.pi * (index % length) / length)


def weighted(terms):
    total = None
    for factor, value in terms:
        if abs(factor) < 1e-12:
            continue
        if abs(factor - 1.0) < 1e-12:
            term = value
        elif abs(factor + 1.0) < 1e-12:
            term = -value
        else:
            term = factor * value
        total = term if total is None else total + term
    return total


def spectrum_kernel(
    screen, image, before, after, pay, table, turn_cos, turn_sin,
    out, slope_x, slope_y, frame, other, folded, packed,
):
    rows, grid = image.shape
    fine = turn_cos.shape[0]
    width = turn_cos.shape[1]
    low = before[...].astype(F32)
    high = after[...].astype(F32)
    frame[0:halo, :] = low[0:halo]
    frame[halo : halo + rows, :] = image[...]
    frame[halo + rows :, :] = high[0:halo]
    other[0:halo, :] = low[halo:]
    other[halo : halo + rows, :] = screen[...]
    other[halo + rows :, :] = high[halo:]
    image_y = slope(frame[...], row_roll)
    slope_y[...] = image_y
    image_x = slope(image[...], lane_roll)
    slope_x[...] = image_x
    change_y = slope(other[...], row_roll) * image_y
    other[...] = change_y
    joined = (
        image[...]
        + slope(screen[...], lane_roll) * image_x
        + other[halo : halo + rows, :]
    )
    tiles = [joined[:, i * width : (i + 1) * width] for i in range(fine)]
    half = fine // 2
    even = [tiles[j] + tiles[fine - j] for j in range(1, half)]
    odd = [tiles[j] - tiles[fine - j] for j in range(1, half)]
    for k in range(half + 1):
        part_real = weighted(
            [(1.0, tiles[0]), ((-1.0) ** k, tiles[half])]
            + [(cosine(j * k, fine), even[j - 1]) for j in range(1, half)]
        )
        part_imag = weighted([(-sine(j * k, fine), odd[j - 1]) for j in range(1, half)])
        for index in sorted({k, (fine - k) % fine}):
            sign = 1.0 if index == k else -1.0
            cos = turn_cos[index : index + 1, :]
            sin = turn_sin[index : index + 1, :]
            lead, trail = part_real * cos, part_real * sin
            if part_imag is None:
                value_real, value_imag = lead, -trail
            else:
                value_real = lead + sign * (part_imag * sin)
                value_imag = sign * (part_imag * cos) - trail
            span = slice(index * rows, (index + 1) * rows)
            folded[span, 0:width] = value_real.astype(BF16)
            folded[span, width:] = value_imag.astype(BF16)
    spectrum = lax.dot_general(table[...], folded[...], NT, preferred_element_type=F32)
    deep = width // 2
    for side in range(2):
        for part in range(2):
            packed[pl.ds(side * 4 + part, deep, stride=8), :] = spectrum[
                part * deep : (part + 1) * deep, side * width : (side + 1) * width
            ]
    packed[pl.ds(2, width, stride=4), :] = pay[...]
    packed[pl.ds(3, width, stride=4), :] = jnp.zeros((width, width), F32)
    out[...] = packed[...].astype(BF16)


def visibility_kernel(
    arrived, coarse, coarse_back, inner, inner_back, turn_cos, turn_sin,
    out, wide, hot, hot_back, spread, *, slots, scale,
):
    width = arrived.shape[1]
    wide[...] = arrived[...].astype(F32)
    part_real = wide[pl.ds(0, width, stride=4), :]
    part_imag = wide[pl.ds(1, width, stride=4), :]
    pay = wide[pl.ds(2, width, stride=4), :]
    pay_back = jnp.transpose(pay)
    stacked = jnp.concatenate([part_real, part_imag], 0).astype(BF16)
    mixed = lax.dot_general(coarse[...], stacked, NN, preferred_element_type=F32)
    cos, sin = turn_cos[...], turn_sin[...]
    left, right = mixed[:width], mixed[width:]
    turned = jnp.concatenate([left * cos + right * sin, right * cos - left * sin], 1)
    cells = scale * lax.dot_general(
        turned.astype(BF16), inner[...], NN, preferred_element_type=F32
    )
    lead = cells.astype(BF16)
    rest = (cells - lead.astype(F32)).astype(BF16)
    across = lax.broadcasted_iota(jnp.int32, (width, width), 1).astype(F32)
    down = lax.broadcasted_iota(jnp.int32, (width, width), 0).astype(F32)
    for slot in range(slots):
        at = slot * fields
        span = slice(slot * width, (slot + 1) * width)
        hot[span, :] = (pay[:, at : at + 1] == across).astype(F32).astype(BF16)
        hot_back[:, span] = (pay_back[at : at + 1, :] == down).astype(F32).astype(BF16)
    picked = lax.dot_general(
        hot[...], lead, NN, preferred_element_type=F32
    ) + lax.dot_general(hot[...], rest, NN, preferred_element_type=F32)
    for slot in range(slots):
        at = slot * fields
        span = slice(slot * width, (slot + 1) * width)
        value = [pay[:, at + i : at + i + 1] for i in range(fields)]
        mask = value[1] == across
        weight = value[6] + value[7]
        for part in range(2):
            model = jnp.sum(
                jnp.where(mask, picked[span, part * width : (part + 1) * width], 0.0),
                axis=1,
                keepdims=True,
            )
            error = weight * (model - (value[2 + 2 * part] + value[3 + 2 * part]))
            spread[span, part * width : (part + 1) * width] = jnp.where(
                mask, error, 0.0
            ).astype(BF16)
    sums = lax.dot_general(hot_back[...], spread[...], NN, preferred_element_type=F32)
    mixed = lax.dot_general(
        sums.astype(BF16), inner_back[...], NN, preferred_element_type=F32
    )
    left, right = mixed[:, :width], mixed[:, width:]
    turned = jnp.concatenate([left * cos - right * sin, right * cos + left * sin], 0)
    back = lax.dot_general(
        coarse_back[...], turned.astype(BF16), NN, preferred_element_type=F32
    )
    fine = 16
    place = jnp.bitwise_and(
        lax.broadcasted_iota(jnp.int32, (width, width), 1), fine - 1
    )
    for part in range(2):
        own = back[part * width : (part + 1) * width]
        wide[pl.ds(part, width, stride=4), :] = own
        wide[pl.ds(2 + part, width, stride=4), :] = jnp.where(
            place >= fine - 2, row_roll(own, 1), jnp.where(place < 2, row_roll(own, -1), 0.0)
        )
    out[...] = wide[...].astype(BF16)


def gradient_kernel(
    arrived, slope_x, slope_y, table, turn_cos, turn_sin,
    out, wide, grouped, frame, *, scale,
):
    rows, grid = slope_x.shape
    fine, width = turn_cos.shape
    deep = width // 2
    half = fine // 2
    wide[...] = arrived[...].astype(F32)
    frame[...] = jnp.zeros(frame.shape, F32)
    main = None
    for kind in (1, 0):
        for side in range(2):
            for part in range(2):
                grouped[
                    part * deep : (part + 1) * deep, side * width : (side + 1) * width
                ] = wide[pl.ds(side * 4 + 2 * kind + part, deep, stride=8), :]
        flat = jnp.transpose(grouped[...]).astype(BF16)
        spread = lax.dot_general(flat, table[...], NN, preferred_element_type=F32)
        real, imag = [], []
        for k in range(fine):
            cos = scale * turn_cos[k : k + 1, :]
            sin = scale * turn_sin[k : k + 1, :]
            left = spread[k * rows : (k + 1) * rows, 0:width]
            right = spread[k * rows : (k + 1) * rows, width:]
            real.append(left * cos - right * sin)
            imag.append(right * cos + left * sin)
        even = [real[k] + real[fine - k] for k in range(1, half)]
        odd = [imag[k] - imag[fine - k] for k in range(1, half)]
        for c in range(half + 1):
            plain = weighted(
                [(1.0, real[0]), ((-1.0) ** c, real[half])]
                + [(cosine(c * k, fine), even[k - 1]) for k in range(1, half)]
            )
            cross = weighted([(sine(c * k, fine), odd[k - 1]) for k in range(1, half)])
            for index in sorted({c, (fine - c) % fine}):
                if cross is None:
                    value = plain
                else:
                    value = plain - cross if index == c else plain + cross
                span = slice(index * width, (index + 1) * width)
                if kind == 1:
                    frame[halo - 2 : halo, span] = value[rows - 2 :]
                    frame[halo + rows : halo + rows + 2, span] = value[0:2]
                else:
                    frame[halo : halo + rows, span] = value
    push_x = frame[halo : halo + rows, :] * slope_x[...]
    frame[...] = -slope(frame[...] * slope_y[...], row_roll)
    out[...] = frame[halo : halo + rows, :] - slope(push_x, lane_roll)


def whole(count):
    return [pl.BlockSpec(memory_space=pltpu.VMEM)] * count


def local(screens, image, vis_row, vis_block, vis_column, vis_real, vis_imag, vis_weight):
    rows, grid = image.shape
    slabs = lax.axis_size("slab")
    owned = grid // 2 // slabs
    slots = 3 * vis_row.shape[0] // slabs
    screen = screens.reshape(rows, grid)
    low, high = tables(rows, slabs, owned, grid)
    row_forward, row_back, coarse, coarse_back, inner, inner_back = low
    col_cos, col_sin, row_cos, row_sin = high
    width = slabs

    ring = [(i, (i + 1) % slabs) for i in range(slabs)]
    tail = jnp.concatenate([image[rows - halo :], screen[rows - halo :]], 0).astype(BF16)
    head = jnp.concatenate([image[:halo], screen[:halo]], 0).astype(BF16)
    before = lax.ppermute(tail, "slab", ring)
    after = lax.ppermute(head, "slab", [(b, a) for a, b in ring])

    line = (1, vis_row.shape[0])
    pay = pl.pallas_call(
        payload_kernel,
        out_shape=jax.ShapeDtypeStruct((slabs, width), F32),
        in_specs=whole(6),
        out_specs=pl.BlockSpec(memory_space=pltpu.VMEM),
        scratch_shapes=[pltpu.VMEM((width, line[1]), F32)],
        cost_estimate=pl.CostEstimate(flops=30_000_000, bytes_accessed=200_000, transcendentals=0),
        name="payload",
    )(
        vis_row.reshape(line), vis_block.reshape(line), vis_column.reshape(line),
        vis_real.reshape(line), vis_imag.reshape(line), vis_weight.reshape(line),
    )
    framed = rows + 2 * halo
    send, slope_x, slope_y = pl.pallas_call(
        spectrum_kernel,
        out_shape=[
            jax.ShapeDtypeStruct((4 * slabs, width), BF16),
            jax.ShapeDtypeStruct((rows, grid), F32),
            jax.ShapeDtypeStruct((framed, grid), F32),
        ],
        in_specs=whole(8),
        out_specs=whole(3),
        scratch_shapes=[
            pltpu.VMEM((framed, grid), F32),
            pltpu.VMEM((framed, grid), F32),
            pltpu.VMEM((2 * width, 2 * width), BF16),
            pltpu.VMEM((4 * slabs, width), F32),
        ],
        name="spectrum",
    )(screen, image, before, after, pay, row_forward, col_cos, col_sin)
    arrived = lax.all_to_all(
        send.reshape(slabs, 4, width), "slab", split_axis=0, concat_axis=0, tiled=True
    ).reshape(4 * slabs, width)
    scale = 1.0 / grid
    back = pl.pallas_call(
        lambda *refs: visibility_kernel(*refs, slots=slots, scale=scale),
        out_shape=jax.ShapeDtypeStruct((4 * slabs, width), BF16),
        in_specs=whole(7),
        out_specs=pl.BlockSpec(memory_space=pltpu.VMEM),
        scratch_shapes=[
            pltpu.VMEM((4 * slabs, width), F32),
            pltpu.VMEM((slots * width, width), BF16),
            pltpu.VMEM((width, slots * width), BF16),
            pltpu.VMEM((slots * width, 2 * width), BF16),
        ],
        name="visibility",
    )(arrived, coarse, coarse_back, inner, inner_back, row_cos, row_sin)
    returned = lax.all_to_all(
        back.reshape(slabs, 4, width), "slab", split_axis=0, concat_axis=0, tiled=True
    ).reshape(4 * slabs, width)
    grad = pl.pallas_call(
        lambda *refs: gradient_kernel(*refs, scale=scale),
        out_shape=jax.ShapeDtypeStruct((rows, grid), F32),
        in_specs=whole(6),
        out_specs=pl.BlockSpec(memory_space=pltpu.VMEM),
        scratch_shapes=[
            pltpu.VMEM((4 * slabs, width), F32),
            pltpu.VMEM((width, 2 * width), F32),
            pltpu.VMEM((framed, grid), F32),
        ],
        name="gradient",
    )(returned, slope_x, slope_y, row_back, col_cos, col_sin)
    return grad.reshape(1, rows, grid)


def solution(mesh):
    in_specs = (
        P(("chain", "vis"), "slab", None),
        P(("chain", "slab"), None),
        P("slab"),
        P("slab", None),
        P("slab"),
        P("slab"),
        P("slab"),
        P("slab"),
    )
    out_specs = P(("chain", "vis"), "slab", None)
    return jax.shard_map(local, mesh=mesh, in_specs=in_specs, out_specs=out_specs, check_vma=False)
```

```python
import math

import jax
import jax.numpy as jnp
import numpy as np
from jax import lax
from jax.experimental import pallas as pl
from jax.experimental.pallas import tpu as pltpu
from jax.sharding import PartitionSpec as P

F32 = jnp.float32
BF16 = jnp.bfloat16
NT = (((1,), (1,)), ((), ()))
NN = (((1,), (0,)), ((), ()))
fields = 8
halo = 4
lead = 2


def angle(first, second, length):
    turn = (np.outer(first, second) % length) * (2.0 * math.pi / length)
    return np.cos(turn), np.sin(turn)


def tables(rows, slabs, owned, grid):
    fine = grid // slabs
    c2, k2, k1 = np.arange(slabs), np.arange(slabs // 2), np.arange(fine)
    shifted = np.arange(rows) - lead
    cos, sin = angle(k2, c2, slabs)
    row_forward = np.block([[cos, sin], [-sin, cos]])
    row_back = np.block([[cos, sin], [-sin, cos]])
    col_turn = angle(k1, c2, grid)
    cos, sin = angle(c2, c2, slabs)
    coarse = np.block([[cos, sin], [-sin, cos]])
    cos, sin = angle(shifted, k1, fine)
    eye = np.eye(owned)
    cos, sin = np.kron(eye, cos), np.kron(eye, sin)
    inner = np.block([[cos, -sin], [sin, cos]])
    row_turn = [np.tile(part, (1, owned)) for part in angle(c2, shifted, grid)]
    low = [row_forward, row_back, coarse, coarse.T, inner, inner.T]
    high = [*col_turn, *row_turn]
    return [jnp.asarray(t, BF16) for t in low], [jnp.asarray(t, F32) for t in high]


def payload_kernel(row, block, column, real, imag, weight, out, wide):
    vis_count = row.shape[1]
    slabs = out.shape[0]
    hot = (
        lax.broadcasted_iota(jnp.int32, (slabs, vis_count), 0) == block[...]
    ).astype(F32)
    hot_low = hot.astype(BF16)
    earlier = (
        lax.broadcasted_iota(jnp.int32, (vis_count, vis_count), 0)
        < lax.broadcasted_iota(jnp.int32, (vis_count, vis_count), 1)
    ).astype(F32).astype(BF16)
    before = lax.dot_general(hot_low, earlier, NN, preferred_element_type=F32)
    rank = jnp.sum(before * hot, axis=0, keepdims=True)
    ky = row[...]
    parts = [
        jnp.bitwise_and(ky, slabs - 1).astype(F32),
        (column[...] * (slabs // 8) + ky // slabs).astype(F32),
    ]
    for value in (real, imag, weight):
        whole = value[...]
        lead = whole.astype(BF16).astype(F32)
        parts += [lead, whole - lead]
    which = lax.broadcasted_iota(jnp.int32, (fields, vis_count), 0)
    stack = jnp.zeros((fields, vis_count), F32)
    for index, part in enumerate(parts):
        stack = jnp.where(which == index, part, stack)
    for slot in range(slabs // fields):
        wide[slot * fields : (slot + 1) * fields, :] = jnp.where(
            rank == float(slot), stack, 0.0
        )
    out[...] = lax.dot_general(
        hot_low, wide[...].astype(BF16), NT, preferred_element_type=F32
    )


def lane_roll(x, shift):
    return pltpu.roll(x, shift % x.shape[1], 1)


def row_roll(x, shift):
    return pltpu.roll(x, shift % x.shape[0], 0)


def slope(x, roll):
    return (8.0 * (roll(x, -1) - roll(x, 1)) - (roll(x, -2) - roll(x, 2))) * (1.0 / 12.0)


def cosine(index, length):
    return math.cos(2.0 * math.pi * (index % length) / length)


def sine(index, length):
    return math.sin(2.0 * math.pi * (index % length) / length)


def weighted(terms):
    total = None
    for factor, value in terms:
        if abs(factor) < 1e-12:
            continue
        if abs(factor - 1.0) < 1e-12:
            term = value
        elif abs(factor + 1.0) < 1e-12:
            term = -value
        else:
            term = factor * value
        total = term if total is None else total + term
    return total


def spectrum_kernel(
    screen, image, before, pay, table, turn_cos, turn_sin,
    out, slope_x, slope_y, frame, other, folded, packed, relayed,
):
    rows, grid = image.shape
    fine, width = turn_cos.shape
    framed = frame.shape[0]
    edge = before[...].astype(F32)
    for index, (ref, own) in enumerate(((frame, image), (other, screen))):
        part = edge[index * halo : (index + 1) * halo]
        ref[0:lead, :] = part[halo - lead :]
        ref[lead : lead + rows, :] = own[...]
        ref[lead + rows : framed - lead, :] = jnp.zeros((framed - rows - 2 * lead, grid), F32)
        ref[framed - lead :, :] = part[: halo - lead]
    field = frame[...]
    image_x = slope(field, lane_roll)
    image_y = slope(field, row_roll)
    slope_x[...] = row_roll(image_x, -lead)[0:rows]
    slope_y[...] = image_y[0:rows]
    for i in range(fine):
        relayed[i * 8 : (i + 1) * 8, :] = image_y[0:8, i * width : (i + 1) * width]
    change = other[...]
    change_x = slope(change[0:rows], lane_roll) * image_x[0:rows]
    joined = field[0:rows] + change_x + (slope(change, row_roll) * image_y)[0:rows]
    tiles = [joined[:, i * width : (i + 1) * width] for i in range(fine)]
    half = fine // 2
    even = [tiles[j] + tiles[fine - j] for j in range(1, half)]
    odd = [tiles[j] - tiles[fine - j] for j in range(1, half)]
    for k in range(half + 1):
        part_real = weighted(
            [(1.0, tiles[0]), ((-1.0) ** k, tiles[half])]
            + [(cosine(j * k, fine), even[j - 1]) for j in range(1, half)]
        )
        part_imag = weighted([(-sine(j * k, fine), odd[j - 1]) for j in range(1, half)])
        for index in sorted({k, (fine - k) % fine}):
            sign = 1.0 if index == k else -1.0
            cos = turn_cos[index : index + 1, :]
            sin = turn_sin[index : index + 1, :]
            first, second = part_real * cos, part_real * sin
            if part_imag is None:
                value_real, value_imag = first, -second
            else:
                value_real = first + sign * (part_imag * sin)
                value_imag = sign * (part_imag * cos) - second
            span = slice(index * rows, (index + 1) * rows)
            folded[span, 0:width] = value_real.astype(BF16)
            folded[span, width:] = value_imag.astype(BF16)
    spectrum = lax.dot_general(table[...], folded[...], NT, preferred_element_type=F32)
    deep = width // 2
    for side in range(2):
        for part in range(2):
            packed[pl.ds(side * 4 + part, deep, stride=8), :] = spectrum[
                part * deep : (part + 1) * deep, side * width : (side + 1) * width
            ]
    packed[pl.ds(2, width, stride=4), :] = pay[...]
    packed[pl.ds(3, width, stride=4), :] = jnp.transpose(relayed[...])
    out[...] = packed[...].astype(BF16)


def visibility_kernel(
    arrived, coarse, coarse_back, inner, inner_back, turn_cos, turn_sin,
    out, wide, hot, spread, *, slots, scale,
):
    width = arrived.shape[1]
    wide[...] = arrived[...].astype(F32)
    part_real = wide[pl.ds(0, width, stride=4), :]
    part_imag = wide[pl.ds(1, width, stride=4), :]
    pay = jnp.transpose(wide[pl.ds(2, width, stride=4), :])
    relayed = wide[pl.ds(3, width, stride=4), :]
    stacked = jnp.concatenate([part_real, part_imag], 0).astype(BF16)
    mixed = lax.dot_general(coarse[...], stacked, NN, preferred_element_type=F32)
    cos, sin = turn_cos[...], turn_sin[...]
    left, right = mixed[:width], mixed[width:]
    turned = jnp.concatenate([left * cos + right * sin, right * cos - left * sin], 1)
    cells = scale * jnp.transpose(
        lax.dot_general(turned.astype(BF16), inner[...], NN, preferred_element_type=F32)
    )
    main = cells.astype(BF16)
    rest = (cells - main.astype(F32)).astype(BF16)
    split = jnp.concatenate([main, rest], 1)
    down = lax.broadcasted_iota(jnp.int32, (width, width), 0).astype(F32)
    for slot in range(slots):
        at = slot * fields
        span = slice(slot * width, (slot + 1) * width)
        one = (pay[at : at + 1, :] == down).astype(F32).astype(BF16)
        hot[0:width, span] = one
        hot[width:, span] = one
    picked = lax.dot_general(split, hot[...], NN, preferred_element_type=F32)
    for slot in range(slots):
        at = slot * fields
        span = slice(slot * width, (slot + 1) * width)
        value = [pay[at + i : at + i + 1, :] for i in range(fields)]
        mask = value[1] == down
        weight = value[6] + value[7]
        for part in range(2):
            model = jnp.sum(
                jnp.where(mask, picked[part * width : (part + 1) * width, span], 0.0),
                axis=0,
                keepdims=True,
            )
            error = weight * (model - (value[2 + 2 * part] + value[3 + 2 * part]))
            spread[part * width : (part + 1) * width, span] = jnp.where(
                mask, error, 0.0
            ).astype(BF16)
    sums = lax.dot_general(
        hot[0:width, :], spread[...], NT, preferred_element_type=F32
    )
    mixed = lax.dot_general(
        sums.astype(BF16), inner_back[...], NN, preferred_element_type=F32
    )
    left, right = mixed[:, :width], mixed[:, width:]
    turned = jnp.concatenate([left * cos - right * sin, right * cos + left * sin], 0)
    back = lax.dot_general(
        coarse_back[...], turned.astype(BF16), NN, preferred_element_type=F32
    )
    place = jnp.bitwise_and(lax.broadcasted_iota(jnp.int32, (width, width), 1), 15)
    real, imag = back[:width], back[width:]
    wide[pl.ds(0, width, stride=4), :] = real
    wide[pl.ds(1, width, stride=4), :] = imag
    wide[pl.ds(2, width, stride=4), :] = jnp.where(
        place < 8, row_roll(real, -1), lane_roll(row_roll(imag, -1), 8)
    )
    wide[pl.ds(3, width, stride=4), :] = row_roll(relayed, -1)
    out[...] = wide[...].astype(BF16)


def gradient_kernel(
    arrived, slope_x, slope_y, table, turn_cos, turn_sin,
    out, wide, grouped, push_x, *, scale,
):
    rows, grid = slope_x.shape
    fine, width = turn_cos.shape
    deep = width // 2
    half = fine // 2
    wide[...] = arrived[...].astype(F32)
    next_y = jnp.transpose(wide[pl.ds(3, width, stride=4), :])
    for side in range(2):
        both = wide[pl.ds(side * 4 + 2, deep, stride=8), :]
        for part in range(2):
            down = slice(part * deep, (part + 1) * deep)
            grouped[down, side * width : (side + 1) * width] = wide[
                pl.ds(side * 4 + part, deep, stride=8), :
            ]
            grouped[down, (2 + side) * width : (3 + side) * width] = (
                both if part == 0 else lane_roll(both, -8)
            )
    flat = jnp.transpose(grouped[...]).astype(BF16)
    mixed = lax.dot_general(flat, table[...], NN, preferred_element_type=F32)
    below = fine * rows
    real, imag = [], []
    for k in range(fine):
        cos = scale * turn_cos[k : k + 1, :]
        sin = scale * turn_sin[k : k + 1, :]
        at = k * rows
        both = jnp.concatenate([mixed[at : at + rows], mixed[below + at : below + at + 8]], 0)
        left, right = both[:, 0:width], both[:, width:]
        real.append(left * cos - right * sin)
        imag.append(right * cos + left * sin)
    even = [real[k] + real[fine - k] for k in range(1, half)]
    odd = [imag[k] - imag[fine - k] for k in range(1, half)]
    for c in range(half + 1):
        plain = weighted(
            [(1.0, real[0]), ((-1.0) ** c, real[half])]
            + [(cosine(c * k, fine), even[k - 1]) for k in range(1, half)]
        )
        cross = weighted([(sine(c * k, fine), odd[k - 1]) for k in range(1, half)])
        for index in sorted({c, (fine - c) % fine}):
            if cross is None:
                value = plain
            else:
                value = plain - cross if index == c else plain + cross
            span = slice(index * width, (index + 1) * width)
            push_x[:, span] = row_roll(value, -lead)[0:rows] * slope_x[:, span]
            push_y = value * jnp.concatenate(
                [slope_y[:, span], next_y[index * 8 : (index + 1) * 8]], 0
            )
            change = 8.0 * (row_roll(push_y, -1) - row_roll(push_y, -3)) - (
                push_y - row_roll(push_y, -4)
            )
            out[:, span] = change[0:rows] * (1.0 / 12.0)
    out[...] = out[...] - slope(push_x[...], lane_roll)


def whole(count):
    return [pl.BlockSpec(memory_space=pltpu.VMEM)] * count


def local(screens, image, vis_row, vis_block, vis_column, vis_real, vis_imag, vis_weight):
    rows, grid = image.shape
    slabs = lax.axis_size("slab")
    owned = grid // 2 // slabs
    slots = 3 * vis_row.shape[0] // slabs
    screen = screens.reshape(rows, grid)
    low, high = tables(rows, slabs, owned, grid)
    row_forward, row_back, coarse, coarse_back, inner, inner_back = low
    col_cos, col_sin, row_cos, row_sin = high
    width = slabs

    ring = [(i, (i + 1) % slabs) for i in range(slabs)]
    tail = jnp.concatenate([image[rows - halo :], screen[rows - halo :]], 0).astype(BF16)
    before = lax.ppermute(tail, "slab", ring)

    line = (1, vis_row.shape[0])
    limit = pltpu.CompilerParams(vmem_limit_bytes=12 * 2**20)
    place = pl.BlockSpec(memory_space=pltpu.VMEM)
    pay = pl.pallas_call(
        payload_kernel,
        out_shape=jax.ShapeDtypeStruct((slabs, width), F32),
        in_specs=whole(6),
        out_specs=place,
        scratch_shapes=[pltpu.VMEM((width, line[1]), F32)],
        compiler_params=limit,
        cost_estimate=pl.CostEstimate(flops=30_000_000, bytes_accessed=200_000, transcendentals=0),
        name="payload",
    )(
        vis_row.reshape(line), vis_block.reshape(line), vis_column.reshape(line),
        vis_real.reshape(line), vis_imag.reshape(line), vis_weight.reshape(line),
    )
    framed = rows + 8
    send, slope_x, slope_y = pl.pallas_call(
        spectrum_kernel,
        out_shape=[
            jax.ShapeDtypeStruct((4 * slabs, width), BF16),
            jax.ShapeDtypeStruct((rows, grid), F32),
            jax.ShapeDtypeStruct((rows, grid), F32),
        ],
        in_specs=whole(7),
        out_specs=whole(3),
        scratch_shapes=[
            pltpu.VMEM((framed, grid), F32),
            pltpu.VMEM((framed, grid), F32),
            pltpu.VMEM((2 * width, 2 * width), BF16),
            pltpu.VMEM((4 * slabs, width), F32),
            pltpu.VMEM((width, width), F32),
        ],
        compiler_params=limit,
        name="spectrum",
    )(screen, image, before, pay, row_forward, col_cos, col_sin)

    def exchange(block):
        return lax.all_to_all(
            block.reshape(slabs, 4, width), "slab", split_axis=0, concat_axis=0, tiled=True
        ).reshape(4 * slabs, width)

    scale = 1.0 / grid
    back = pl.pallas_call(
        lambda *refs: visibility_kernel(*refs, slots=slots, scale=scale),
        out_shape=jax.ShapeDtypeStruct((4 * slabs, width), BF16),
        in_specs=whole(7),
        out_specs=place,
        scratch_shapes=[
            pltpu.VMEM((4 * slabs, width), F32),
            pltpu.VMEM((2 * width, slots * width), BF16),
            pltpu.VMEM((2 * width, slots * width), BF16),
        ],
        compiler_params=limit,
        name="visibility",
    )(exchange(send), coarse, coarse_back, inner, inner_back, row_cos, row_sin)
    grad = pl.pallas_call(
        lambda *refs: gradient_kernel(*refs, scale=scale),
        out_shape=jax.ShapeDtypeStruct((rows, grid), F32),
        in_specs=whole(6),
        out_specs=place,
        scratch_shapes=[
            pltpu.VMEM((4 * slabs, width), F32),
            pltpu.VMEM((width, 4 * width), F32),
            pltpu.VMEM((rows, grid), F32),
        ],
        compiler_params=limit,
        name="gradient",
    )(exchange(back), slope_x, slope_y, row_back, col_cos, col_sin)
    return grad.reshape(1, rows, grid)


def solution(mesh):
    in_specs = (
        P(("chain", "vis"), "slab", None),
        P(("chain", "slab"), None),
        P("slab"),
        P("slab", None),
        P("slab"),
        P("slab"),
        P("slab"),
        P("slab"),
    )
    out_specs = P(("chain", "vis"), "slab", None)
    return jax.shard_map(local, mesh=mesh, in_specs=in_specs, out_specs=out_specs, check_vma=False)
```

```python
import math

import jax
import jax.numpy as jnp
import numpy as np
from jax import lax
from jax.experimental import pallas as pl
from jax.experimental.pallas import tpu as pltpu
from jax.sharding import PartitionSpec as P

F32 = jnp.float32
BF16 = jnp.bfloat16
NT = (((1,), (1,)), ((), ()))
NN = (((1,), (0,)), ((), ()))
fields = 8
halo = 4
lead = 2


def angle(first, second, length):
    turn = (np.outer(first, second) % length) * (2.0 * math.pi / length)
    return np.cos(turn), np.sin(turn)


def tables(rows, slabs, owned, grid):
    fine = grid // slabs
    c2, k2, k1 = np.arange(slabs), np.arange(slabs // 2), np.arange(fine)
    shifted = np.arange(rows) - lead
    cos, sin = angle(k2, c2, slabs)
    row_forward = np.block([[cos, sin], [-sin, cos]])
    row_back = np.block([[cos, sin], [-sin, cos]])
    col_turn = angle(k1, c2, grid)
    cos, sin = angle(c2, c2, slabs)
    coarse = np.block([[cos, sin], [-sin, cos]])
    cos, sin = angle(shifted, k1, fine)
    eye = np.eye(owned)
    cos, sin = np.kron(eye, cos), np.kron(eye, sin)
    inner = np.block([[cos, -sin], [sin, cos]])
    row_turn = [np.tile(part, (1, owned)) for part in angle(c2, shifted, grid)]
    low = [row_forward, row_back, coarse, coarse.T, inner, inner.T]
    high = [*col_turn, *row_turn]
    return [jnp.asarray(t, BF16) for t in low], [jnp.asarray(t, F32) for t in high]


def payload_kernel(row, block, column, real, imag, weight, out, wide):
    vis_count = row.shape[1]
    slabs = out.shape[0]
    hot = (
        lax.broadcasted_iota(jnp.int32, (slabs, vis_count), 0) == block[...]
    ).astype(F32)
    hot_low = hot.astype(BF16)
    earlier = (
        lax.broadcasted_iota(jnp.int32, (vis_count, vis_count), 0)
        < lax.broadcasted_iota(jnp.int32, (vis_count, vis_count), 1)
    ).astype(F32).astype(BF16)
    before = lax.dot_general(hot_low, earlier, NN, preferred_element_type=F32)
    rank = jnp.sum(before * hot, axis=0, keepdims=True)
    ky = row[...]
    parts = [
        jnp.bitwise_and(ky, slabs - 1).astype(F32),
        (column[...] * (slabs // 8) + ky // slabs).astype(F32),
    ]
    for value in (real, imag, weight):
        whole = value[...]
        lead = whole.astype(BF16).astype(F32)
        parts += [lead, whole - lead]
    which = lax.broadcasted_iota(jnp.int32, (fields, vis_count), 0)
    stack = jnp.zeros((fields, vis_count), F32)
    for index, part in enumerate(parts):
        stack = jnp.where(which == index, part, stack)
    for slot in range(slabs // fields):
        wide[slot * fields : (slot + 1) * fields, :] = jnp.where(
            rank == float(slot), stack, 0.0
        )
    out[...] = lax.dot_general(
        hot_low, wide[...].astype(BF16), NT, preferred_element_type=F32
    )


def lane_roll(x, shift):
    return pltpu.roll(x, shift % x.shape[1], 1)


def row_roll(x, shift):
    return pltpu.roll(x, shift % x.shape[0], 0)


def slope(x, roll):
    return (8.0 * (roll(x, -1) - roll(x, 1)) - (roll(x, -2) - roll(x, 2))) * (1.0 / 12.0)


def cosine(index, length):
    return math.cos(2.0 * math.pi * (index % length) / length)


def sine(index, length):
    return math.sin(2.0 * math.pi * (index % length) / length)


def weighted(terms):
    total = None
    for factor, value in terms:
        if abs(factor) < 1e-12:
            continue
        if abs(factor - 1.0) < 1e-12:
            term = value
        elif abs(factor + 1.0) < 1e-12:
            term = -value
        else:
            term = factor * value
        total = term if total is None else total + term
    return total


def tail_kernel(image, screen, image_kept, screen_kept, tail, done):
    rows = image.shape[0]
    middle = rows // 2
    moves = []
    for first, last in ((middle, rows), (0, middle)):
        for source, target in ((image, image_kept), (screen, screen_kept)):
            move = pltpu.make_async_copy(
                source.at[first:last, :], target.at[first:last, :], done.at[len(moves)]
            )
            move.start()
            moves.append(move)
    moves[0].wait()
    moves[1].wait()
    tail[...] = jnp.concatenate(
        [image_kept[rows - halo :, :], screen_kept[rows - halo :, :]], 0
    ).astype(BF16)
    moves[2].wait()
    moves[3].wait()


def spectrum_kernel(
    screen, image, before, pay, table, turn_cos, turn_sin,
    out, slope_x, slope_y, frame, other, folded, packed, relayed,
):
    rows, grid = image.shape
    fine, width = turn_cos.shape
    framed = frame.shape[0]
    edge = before[...].astype(F32)
    for index, (ref, own) in enumerate(((frame, image), (other, screen))):
        part = edge[index * halo : (index + 1) * halo]
        ref[0:lead, :] = part[halo - lead :]
        ref[lead : lead + rows, :] = own[...]
        ref[lead + rows : framed - lead, :] = jnp.zeros((framed - rows - 2 * lead, grid), F32)
        ref[framed - lead :, :] = part[: halo - lead]
    field = frame[...]
    image_x = slope(field, lane_roll)
    image_y = slope(field, row_roll)
    slope_x[...] = row_roll(image_x, -lead)[0:rows]
    slope_y[...] = image_y[0:rows]
    for i in range(fine):
        relayed[i * 8 : (i + 1) * 8, :] = image_y[0:8, i * width : (i + 1) * width]
    change = other[...]
    change_x = slope(change[0:rows], lane_roll) * image_x[0:rows]
    joined = field[0:rows] + change_x + (slope(change, row_roll) * image_y)[0:rows]
    tiles = [joined[:, i * width : (i + 1) * width] for i in range(fine)]
    half = fine // 2
    even = [tiles[j] + tiles[fine - j] for j in range(1, half)]
    odd = [tiles[j] - tiles[fine - j] for j in range(1, half)]
    for k in range(half + 1):
        part_real = weighted(
            [(1.0, tiles[0]), ((-1.0) ** k, tiles[half])]
            + [(cosine(j * k, fine), even[j - 1]) for j in range(1, half)]
        )
        part_imag = weighted([(-sine(j * k, fine), odd[j - 1]) for j in range(1, half)])
        for index in sorted({k, (fine - k) % fine}):
            sign = 1.0 if index == k else -1.0
            cos = turn_cos[index : index + 1, :]
            sin = turn_sin[index : index + 1, :]
            first, second = part_real * cos, part_real * sin
            if part_imag is None:
                value_real, value_imag = first, -second
            else:
                value_real = first + sign * (part_imag * sin)
                value_imag = sign * (part_imag * cos) - second
            span = slice(index * rows, (index + 1) * rows)
            folded[span, 0:width] = value_real.astype(BF16)
            folded[span, width:] = value_imag.astype(BF16)
    spectrum = lax.dot_general(table[...], folded[...], NT, preferred_element_type=F32)
    deep = width // 2
    for side in range(2):
        for part in range(2):
            packed[pl.ds(side * 4 + part, deep, stride=8), :] = spectrum[
                part * deep : (part + 1) * deep, side * width : (side + 1) * width
            ]
    packed[pl.ds(2, width, stride=4), :] = pay[...]
    packed[pl.ds(3, width, stride=4), :] = jnp.transpose(relayed[...])
    out[...] = packed[...].astype(BF16)


def visibility_kernel(
    arrived, coarse, coarse_back, inner, inner_back, turn_cos, turn_sin,
    out, wide, hot, spread, *, slots, scale,
):
    width = arrived.shape[1]
    wide[...] = arrived[...].astype(F32)
    part_real = wide[pl.ds(0, width, stride=4), :]
    part_imag = wide[pl.ds(1, width, stride=4), :]
    pay = jnp.transpose(wide[pl.ds(2, width, stride=4), :])
    relayed = wide[pl.ds(3, width, stride=4), :]
    stacked = jnp.concatenate([part_real, part_imag], 0).astype(BF16)
    mixed = lax.dot_general(coarse[...], stacked, NN, preferred_element_type=F32)
    cos, sin = turn_cos[...], turn_sin[...]
    left, right = mixed[:width], mixed[width:]
    turned = jnp.concatenate([left * cos + right * sin, right * cos - left * sin], 1)
    cells = scale * jnp.transpose(
        lax.dot_general(turned.astype(BF16), inner[...], NN, preferred_element_type=F32)
    )
    main = cells.astype(BF16)
    rest = (cells - main.astype(F32)).astype(BF16)
    split = jnp.concatenate([main, rest], 1)
    down = lax.broadcasted_iota(jnp.int32, (width, width), 0).astype(F32)
    for slot in range(slots):
        at = slot * fields
        span = slice(slot * width, (slot + 1) * width)
        one = (pay[at : at + 1, :] == down).astype(F32).astype(BF16)
        hot[0:width, span] = one
        hot[width:, span] = one
    picked = lax.dot_general(split, hot[...], NN, preferred_element_type=F32)
    for slot in range(slots):
        at = slot * fields
        span = slice(slot * width, (slot + 1) * width)
        value = [pay[at + i : at + i + 1, :] for i in range(fields)]
        mask = value[1] == down
        weight = value[6] + value[7]
        for part in range(2):
            model = jnp.sum(
                jnp.where(mask, picked[part * width : (part + 1) * width, span], 0.0),
                axis=0,
                keepdims=True,
            )
            error = weight * (model - (value[2 + 2 * part] + value[3 + 2 * part]))
            spread[part * width : (part + 1) * width, span] = jnp.where(
                mask, error, 0.0
            ).astype(BF16)
    sums = lax.dot_general(
        hot[0:width, :], spread[...], NT, preferred_element_type=F32
    )
    mixed = lax.dot_general(
        sums.astype(BF16), inner_back[...], NN, preferred_element_type=F32
    )
    left, right = mixed[:, :width], mixed[:, width:]
    turned = jnp.concatenate([left * cos - right * sin, right * cos + left * sin], 0)
    back = lax.dot_general(
        coarse_back[...], turned.astype(BF16), NN, preferred_element_type=F32
    )
    place = jnp.bitwise_and(lax.broadcasted_iota(jnp.int32, (width, width), 1), 15)
    real, imag = back[:width], back[width:]
    wide[pl.ds(0, width, stride=4), :] = real
    wide[pl.ds(1, width, stride=4), :] = imag
    wide[pl.ds(2, width, stride=4), :] = jnp.where(
        place < 8, row_roll(real, -1), lane_roll(row_roll(imag, -1), 8)
    )
    wide[pl.ds(3, width, stride=4), :] = row_roll(relayed, -1)
    out[...] = wide[...].astype(BF16)


def gradient_kernel(
    arrived, slope_x, slope_y, table, turn_cos, turn_sin,
    out, wide, grouped, push_x, *, scale,
):
    rows, grid = slope_x.shape
    fine, width = turn_cos.shape
    deep = width // 2
    half = fine // 2
    wide[...] = arrived[...].astype(F32)
    next_y = jnp.transpose(wide[pl.ds(3, width, stride=4), :])
    for side in range(2):
        both = wide[pl.ds(side * 4 + 2, deep, stride=8), :]
        for part in range(2):
            down = slice(part * deep, (part + 1) * deep)
            grouped[down, side * width : (side + 1) * width] = wide[
                pl.ds(side * 4 + part, deep, stride=8), :
            ]
            grouped[down, (2 + side) * width : (3 + side) * width] = (
                both if part == 0 else lane_roll(both, -8)
            )
    flat = jnp.transpose(grouped[...]).astype(BF16)
    mixed = lax.dot_general(flat, table[...], NN, preferred_element_type=F32)
    below = fine * rows
    real, imag = [], []
    for k in range(fine):
        cos = scale * turn_cos[k : k + 1, :]
        sin = scale * turn_sin[k : k + 1, :]
        at = k * rows
        both = jnp.concatenate([mixed[at : at + rows], mixed[below + at : below + at + 8]], 0)
        left, right = both[:, 0:width], both[:, width:]
        real.append(left * cos - right * sin)
        imag.append(right * cos + left * sin)
    even = [real[k] + real[fine - k] for k in range(1, half)]
    odd = [imag[k] - imag[fine - k] for k in range(1, half)]
    for c in range(half + 1):
        plain = weighted(
            [(1.0, real[0]), ((-1.0) ** c, real[half])]
            + [(cosine(c * k, fine), even[k - 1]) for k in range(1, half)]
        )
        cross = weighted([(sine(c * k, fine), odd[k - 1]) for k in range(1, half)])
        for index in sorted({c, (fine - c) % fine}):
            if cross is None:
                value = plain
            else:
                value = plain - cross if index == c else plain + cross
            span = slice(index * width, (index + 1) * width)
            push_x[:, span] = row_roll(value, -lead)[0:rows] * slope_x[:, span]
            push_y = value * jnp.concatenate(
                [slope_y[:, span], next_y[index * 8 : (index + 1) * 8]], 0
            )
            change = 8.0 * (row_roll(push_y, -1) - row_roll(push_y, -3)) - (
                push_y - row_roll(push_y, -4)
            )
            out[:, span] = change[0:rows] * (1.0 / 12.0)
    out[...] = out[...] - slope(push_x[...], lane_roll)


def whole(count):
    return [pl.BlockSpec(memory_space=pltpu.VMEM)] * count


def local(screens, image, vis_row, vis_block, vis_column, vis_real, vis_imag, vis_weight):
    rows, grid = image.shape
    slabs = lax.axis_size("slab")
    owned = grid // 2 // slabs
    slots = 3 * vis_row.shape[0] // slabs
    screen = screens.reshape(rows, grid)
    low, high = tables(rows, slabs, owned, grid)
    row_forward, row_back, coarse, coarse_back, inner, inner_back = low
    col_cos, col_sin, row_cos, row_sin = high
    width = slabs

    ring = [(i, (i + 1) % slabs) for i in range(slabs)]
    limit = pltpu.CompilerParams(vmem_limit_bytes=12 * 2**20)
    field = jax.ShapeDtypeStruct((rows, grid), F32)
    image, screen, tail = pl.pallas_call(
        tail_kernel,
        out_shape=[field, field, jax.ShapeDtypeStruct((2 * halo, grid), BF16)],
        in_specs=[pl.BlockSpec(memory_space=pltpu.HBM)] * 2,
        out_specs=whole(3),
        scratch_shapes=[pltpu.SemaphoreType.DMA((4,))],
        compiler_params=limit,
        name="tail",
    )(*(pltpu.with_memory_space_constraint(part, pltpu.HBM) for part in (image, screen)))
    before = lax.ppermute(tail, "slab", ring)

    line = (1, vis_row.shape[0])
    place = pl.BlockSpec(memory_space=pltpu.VMEM)
    pay = pl.pallas_call(
        payload_kernel,
        out_shape=jax.ShapeDtypeStruct((slabs, width), F32),
        in_specs=whole(6),
        out_specs=place,
        scratch_shapes=[pltpu.VMEM((width, line[1]), F32)],
        compiler_params=limit,
        cost_estimate=pl.CostEstimate(flops=30_000_000, bytes_accessed=200_000, transcendentals=0),
        name="payload",
    )(
        vis_row.reshape(line), vis_block.reshape(line), vis_column.reshape(line),
        vis_real.reshape(line), vis_imag.reshape(line), vis_weight.reshape(line),
    )
    framed = rows + 8
    send, slope_x, slope_y = pl.pallas_call(
        spectrum_kernel,
        out_shape=[
            jax.ShapeDtypeStruct((4 * slabs, width), BF16),
            jax.ShapeDtypeStruct((rows, grid), F32),
            jax.ShapeDtypeStruct((rows, grid), F32),
        ],
        in_specs=whole(7),
        out_specs=whole(3),
        scratch_shapes=[
            pltpu.VMEM((framed, grid), F32),
            pltpu.VMEM((framed, grid), F32),
            pltpu.VMEM((2 * width, 2 * width), BF16),
            pltpu.VMEM((4 * slabs, width), F32),
            pltpu.VMEM((width, width), F32),
        ],
        compiler_params=limit,
        name="spectrum",
    )(screen, image, before, pay, row_forward, col_cos, col_sin)

    def exchange(block):
        return lax.all_to_all(
            block.reshape(slabs, 4, width), "slab", split_axis=0, concat_axis=0, tiled=True
        ).reshape(4 * slabs, width)

    scale = 1.0 / grid
    back = pl.pallas_call(
        lambda *refs: visibility_kernel(*refs, slots=slots, scale=scale),
        out_shape=jax.ShapeDtypeStruct((4 * slabs, width), BF16),
        in_specs=whole(7),
        out_specs=place,
        scratch_shapes=[
            pltpu.VMEM((4 * slabs, width), F32),
            pltpu.VMEM((2 * width, slots * width), BF16),
            pltpu.VMEM((2 * width, slots * width), BF16),
        ],
        compiler_params=limit,
        name="visibility",
    )(exchange(send), coarse, coarse_back, inner, inner_back, row_cos, row_sin)
    grad = pl.pallas_call(
        lambda *refs: gradient_kernel(*refs, scale=scale),
        out_shape=jax.ShapeDtypeStruct((rows, grid), F32),
        in_specs=whole(6),
        out_specs=place,
        scratch_shapes=[
            pltpu.VMEM((4 * slabs, width), F32),
            pltpu.VMEM((width, 4 * width), F32),
            pltpu.VMEM((rows, grid), F32),
        ],
        compiler_params=limit,
        name="gradient",
    )(exchange(back), slope_x, slope_y, row_back, col_cos, col_sin)
    return grad.reshape(1, rows, grid)


def solution(mesh):
    in_specs = (
        P(("chain", "vis"), "slab", None),
        P(("chain", "slab"), None),
        P("slab"),
        P("slab", None),
        P("slab"),
        P("slab"),
        P("slab"),
        P("slab"),
    )
    out_specs = P(("chain", "vis"), "slab", None)
    return jax.shard_map(local, mesh=mesh, in_specs=in_specs, out_specs=out_specs, check_vma=False)
```

```python
import math

import jax
import jax.numpy as jnp
import numpy as np
from jax import lax
from jax.experimental import pallas as pl
from jax.experimental.pallas import tpu as pltpu
from jax.sharding import PartitionSpec as P

F32 = jnp.float32
BF16 = jnp.bfloat16
NT = (((1,), (1,)), ((), ()))
NN = (((1,), (0,)), ((), ()))
fields = 8
halo = 4
lead = 2


def angle(first, second, length):
    turn = (np.outer(first, second) % length) * (2.0 * math.pi / length)
    return np.cos(turn), np.sin(turn)


def tables(rows, slabs, owned, grid):
    fine = grid // slabs
    c2, k2, k1 = np.arange(slabs), np.arange(slabs // 2), np.arange(fine)
    shifted = np.arange(rows) - lead
    cos, sin = angle(k2, c2, slabs)
    row_forward = np.block([[cos, sin], [-sin, cos]])
    row_back = np.block([[cos, sin], [-sin, cos]])
    col_turn = angle(k1, c2, grid)
    cos, sin = angle(c2, c2, slabs)
    coarse = np.block([[cos, sin], [-sin, cos]])
    cos, sin = angle(shifted, k1, fine)
    eye = np.eye(owned)
    cos, sin = np.kron(eye, cos), np.kron(eye, sin)
    inner = np.block([[cos, -sin], [sin, cos]])
    row_turn = [np.tile(part, (1, owned)) for part in angle(c2, shifted, grid)]
    low = [row_forward, row_back, coarse, coarse.T, inner, inner.T]
    high = [*col_turn, *row_turn]
    return [jnp.asarray(t, BF16) for t in low], [jnp.asarray(t, F32) for t in high]


def payload_kernel(
    image, screen, row, block, column, real, imag, weight,
    out, image_kept, screen_kept, base, slope_x, wide, done,
):
    moves = [
        pltpu.make_async_copy(source, target, done.at[index])
        for index, (source, target) in enumerate(
            ((image, image_kept), (screen, screen_kept))
        )
    ]
    for move in moves:
        move.start()
    vis_count = row.shape[1]
    slabs = out.shape[0]
    hot = (
        lax.broadcasted_iota(jnp.int32, (slabs, vis_count), 0) == block[...]
    ).astype(F32)
    hot_low = hot.astype(BF16)
    earlier = (
        lax.broadcasted_iota(jnp.int32, (vis_count, vis_count), 0)
        < lax.broadcasted_iota(jnp.int32, (vis_count, vis_count), 1)
    ).astype(F32).astype(BF16)
    before = lax.dot_general(hot_low, earlier, NN, preferred_element_type=F32)
    rank = jnp.sum(before * hot, axis=0, keepdims=True)
    ky = row[...]
    parts = [
        jnp.bitwise_and(ky, slabs - 1).astype(F32),
        (column[...] * (slabs // 8) + ky // slabs).astype(F32),
    ]
    for value in (real, imag, weight):
        whole = value[...]
        lead = whole.astype(BF16).astype(F32)
        parts += [lead, whole - lead]
    which = lax.broadcasted_iota(jnp.int32, (fields, vis_count), 0)
    stack = jnp.zeros((fields, vis_count), F32)
    for index, part in enumerate(parts):
        stack = jnp.where(which == index, part, stack)
    for slot in range(slabs // fields):
        wide[slot * fields : (slot + 1) * fields, :] = jnp.where(
            rank == float(slot), stack, 0.0
        )
    out[...] = lax.dot_general(
        hot_low, wide[...].astype(BF16), NT, preferred_element_type=F32
    )
    for move in moves:
        move.wait()
    own = image_kept[...]
    own_x = slope(own, lane_roll)
    slope_x[...] = own_x
    base[...] = own + slope(screen_kept[...], lane_roll) * own_x


def lane_roll(x, shift):
    return pltpu.roll(x, shift % x.shape[1], 1)


def row_roll(x, shift):
    return pltpu.roll(x, shift % x.shape[0], 0)


def slope(x, roll):
    return (8.0 * (roll(x, -1) - roll(x, 1)) - (roll(x, -2) - roll(x, 2))) * (1.0 / 12.0)


def cosine(index, length):
    return math.cos(2.0 * math.pi * (index % length) / length)


def sine(index, length):
    return math.sin(2.0 * math.pi * (index % length) / length)


def weighted(terms):
    total = None
    for factor, value in terms:
        if abs(factor) < 1e-12:
            continue
        if abs(factor - 1.0) < 1e-12:
            term = value
        elif abs(factor + 1.0) < 1e-12:
            term = -value
        else:
            term = factor * value
        total = term if total is None else total + term
    return total


def tail_kernel(image, screen, tail, kept, done):
    rows, grid = image.shape
    below, span = rows - 8, grid // 2
    moves = []
    for index, source in enumerate((image, screen)):
        for side in range(2):
            columns = slice(side * span, (side + 1) * span)
            moves.append(
                pltpu.make_async_copy(
                    source.at[below:rows, columns],
                    kept.at[index * 8 : (index + 1) * 8, columns],
                    done.at[len(moves)],
                )
            )
            moves[-1].start()
    for move in moves:
        move.wait()
    tail[...] = jnp.concatenate(
        [kept[8 - halo : 8, :], kept[16 - halo : 16, :]], 0
    ).astype(BF16)


def spectrum_kernel(
    screen, image, base, before, pay, table, turn_cos, turn_sin,
    out, slope_y, frame, other, joint, folded, packed, relayed,
):
    rows, grid = image.shape
    fine, width = turn_cos.shape
    framed = frame.shape[0]
    edge = before[...].astype(F32)
    for index, (ref, own) in enumerate(((frame, image), (other, screen))):
        part = edge[index * halo : (index + 1) * halo]
        ref[0:lead, :] = part[halo - lead :]
        ref[lead : lead + rows, :] = own[...]
        ref[lead + rows : framed - lead, :] = jnp.zeros((framed - rows - 2 * lead, grid), F32)
        ref[framed - lead :, :] = part[: halo - lead]
    edge_x = slope(edge, lane_roll)
    edge_base = edge[0:halo] + edge_x[halo:] * edge_x[0:halo]
    joint[0:lead, :] = edge_base[halo - lead :]
    joint[lead:, :] = base[0 : rows - lead, :]
    image_y = slope(frame[...], row_roll)
    slope_y[...] = image_y[0:rows]
    for i in range(fine):
        relayed[i * 8 : (i + 1) * 8, :] = image_y[0:8, i * width : (i + 1) * width]
    joined = joint[...] + (slope(other[...], row_roll) * image_y)[0:rows]
    tiles = [joined[:, i * width : (i + 1) * width] for i in range(fine)]
    half = fine // 2
    even = [tiles[j] + tiles[fine - j] for j in range(1, half)]
    odd = [tiles[j] - tiles[fine - j] for j in range(1, half)]
    for k in range(half + 1):
        part_real = weighted(
            [(1.0, tiles[0]), ((-1.0) ** k, tiles[half])]
            + [(cosine(j * k, fine), even[j - 1]) for j in range(1, half)]
        )
        part_imag = weighted([(-sine(j * k, fine), odd[j - 1]) for j in range(1, half)])
        for index in sorted({k, (fine - k) % fine}):
            sign = 1.0 if index == k else -1.0
            cos = turn_cos[index : index + 1, :]
            sin = turn_sin[index : index + 1, :]
            first, second = part_real * cos, part_real * sin
            if part_imag is None:
                value_real, value_imag = first, -second
            else:
                value_real = first + sign * (part_imag * sin)
                value_imag = sign * (part_imag * cos) - second
            span = slice(index * rows, (index + 1) * rows)
            folded[span, 0:width] = value_real.astype(BF16)
            folded[span, width:] = value_imag.astype(BF16)
    spectrum = lax.dot_general(table[...], folded[...], NT, preferred_element_type=F32)
    deep = width // 2
    for side in range(2):
        for part in range(2):
            packed[pl.ds(side * 4 + part, deep, stride=8), :] = spectrum[
                part * deep : (part + 1) * deep, side * width : (side + 1) * width
            ]
    packed[pl.ds(2, width, stride=4), :] = pay[...]
    packed[pl.ds(3, width, stride=4), :] = jnp.transpose(relayed[...])
    out[...] = packed[...].astype(BF16)


def visibility_kernel(
    arrived, coarse, coarse_back, inner, inner_back, turn_cos, turn_sin,
    out, wide, hot, spread, *, slots, scale,
):
    width = arrived.shape[1]
    wide[...] = arrived[...].astype(F32)
    part_real = wide[pl.ds(0, width, stride=4), :]
    part_imag = wide[pl.ds(1, width, stride=4), :]
    pay = jnp.transpose(wide[pl.ds(2, width, stride=4), :])
    relayed = wide[pl.ds(3, width, stride=4), :]
    stacked = jnp.concatenate([part_real, part_imag], 0).astype(BF16)
    mixed = lax.dot_general(coarse[...], stacked, NN, preferred_element_type=F32)
    cos, sin = turn_cos[...], turn_sin[...]
    left, right = mixed[:width], mixed[width:]
    turned = jnp.concatenate([left * cos + right * sin, right * cos - left * sin], 1)
    cells = scale * jnp.transpose(
        lax.dot_general(turned.astype(BF16), inner[...], NN, preferred_element_type=F32)
    )
    main = cells.astype(BF16)
    rest = (cells - main.astype(F32)).astype(BF16)
    split = jnp.concatenate([main, rest], 1)
    down = lax.broadcasted_iota(jnp.int32, (width, width), 0).astype(F32)
    for slot in range(slots):
        at = slot * fields
        span = slice(slot * width, (slot + 1) * width)
        one = (pay[at : at + 1, :] == down).astype(F32).astype(BF16)
        hot[0:width, span] = one
        hot[width:, span] = one
    picked = lax.dot_general(split, hot[...], NN, preferred_element_type=F32)
    for slot in range(slots):
        at = slot * fields
        span = slice(slot * width, (slot + 1) * width)
        value = [pay[at + i : at + i + 1, :] for i in range(fields)]
        mask = value[1] == down
        weight = value[6] + value[7]
        for part in range(2):
            model = jnp.sum(
                jnp.where(mask, picked[part * width : (part + 1) * width, span], 0.0),
                axis=0,
                keepdims=True,
            )
            error = weight * (model - (value[2 + 2 * part] + value[3 + 2 * part]))
            spread[part * width : (part + 1) * width, span] = jnp.where(
                mask, error, 0.0
            ).astype(BF16)
    sums = lax.dot_general(
        hot[0:width, :], spread[...], NT, preferred_element_type=F32
    )
    mixed = lax.dot_general(
        sums.astype(BF16), inner_back[...], NN, preferred_element_type=F32
    )
    left, right = mixed[:, :width], mixed[:, width:]
    turned = jnp.concatenate([left * cos - right * sin, right * cos + left * sin], 0)
    back = lax.dot_general(
        coarse_back[...], turned.astype(BF16), NN, preferred_element_type=F32
    )
    place = jnp.bitwise_and(lax.broadcasted_iota(jnp.int32, (width, width), 1), 15)
    real, imag = back[:width], back[width:]
    wide[pl.ds(0, width, stride=4), :] = real
    wide[pl.ds(1, width, stride=4), :] = imag
    wide[pl.ds(2, width, stride=4), :] = jnp.where(
        place < 8, row_roll(real, -1), lane_roll(row_roll(imag, -1), 8)
    )
    wide[pl.ds(3, width, stride=4), :] = row_roll(relayed, -1)
    out[...] = wide[...].astype(BF16)


def gradient_kernel(
    arrived, slope_x, slope_y, table, turn_cos, turn_sin,
    out, wide, grouped, push_x, *, scale,
):
    rows, grid = slope_x.shape
    fine, width = turn_cos.shape
    deep = width // 2
    half = fine // 2
    wide[...] = arrived[...].astype(F32)
    next_y = jnp.transpose(wide[pl.ds(3, width, stride=4), :])
    for side in range(2):
        both = wide[pl.ds(side * 4 + 2, deep, stride=8), :]
        for part in range(2):
            down = slice(part * deep, (part + 1) * deep)
            grouped[down, side * width : (side + 1) * width] = wide[
                pl.ds(side * 4 + part, deep, stride=8), :
            ]
            grouped[down, (2 + side) * width : (3 + side) * width] = (
                both if part == 0 else lane_roll(both, -8)
            )
    flat = jnp.transpose(grouped[...]).astype(BF16)
    mixed = lax.dot_general(flat, table[...], NN, preferred_element_type=F32)
    below = fine * rows
    real, imag = [], []
    for k in range(fine):
        cos = scale * turn_cos[k : k + 1, :]
        sin = scale * turn_sin[k : k + 1, :]
        at = k * rows
        both = jnp.concatenate([mixed[at : at + rows], mixed[below + at : below + at + 8]], 0)
        left, right = both[:, 0:width], both[:, width:]
        real.append(left * cos - right * sin)
        imag.append(right * cos + left * sin)
    even = [real[k] + real[fine - k] for k in range(1, half)]
    odd = [imag[k] - imag[fine - k] for k in range(1, half)]
    for c in range(half + 1):
        plain = weighted(
            [(1.0, real[0]), ((-1.0) ** c, real[half])]
            + [(cosine(c * k, fine), even[k - 1]) for k in range(1, half)]
        )
        cross = weighted([(sine(c * k, fine), odd[k - 1]) for k in range(1, half)])
        for index in sorted({c, (fine - c) % fine}):
            if cross is None:
                value = plain
            else:
                value = plain - cross if index == c else plain + cross
            span = slice(index * width, (index + 1) * width)
            push_x[:, span] = row_roll(value, -lead)[0:rows] * slope_x[:, span]
            push_y = value * jnp.concatenate(
                [slope_y[:, span], next_y[index * 8 : (index + 1) * 8]], 0
            )
            change = 8.0 * (row_roll(push_y, -1) - row_roll(push_y, -3)) - (
                push_y - row_roll(push_y, -4)
            )
            out[:, span] = change[0:rows] * (1.0 / 12.0)
    out[...] = out[...] - slope(push_x[...], lane_roll)


def whole(count):
    return [pl.BlockSpec(memory_space=pltpu.VMEM)] * count


def local(screens, image, vis_row, vis_block, vis_column, vis_real, vis_imag, vis_weight):
    rows, grid = image.shape
    slabs = lax.axis_size("slab")
    owned = grid // 2 // slabs
    slots = 3 * vis_row.shape[0] // slabs
    screen = screens.reshape(rows, grid)
    low, high = tables(rows, slabs, owned, grid)
    row_forward, row_back, coarse, coarse_back, inner, inner_back = low
    col_cos, col_sin, row_cos, row_sin = high
    width = slabs

    ring = [(i, (i + 1) % slabs) for i in range(slabs)]
    limit = pltpu.CompilerParams(vmem_limit_bytes=12 * 2**20)
    field = jax.ShapeDtypeStruct((rows, grid), F32)
    far = [pl.BlockSpec(memory_space=pltpu.HBM)] * 2
    image, screen = (
        pltpu.with_memory_space_constraint(part, pltpu.HBM) for part in (image, screen)
    )
    tail = pl.pallas_call(
        tail_kernel,
        out_shape=jax.ShapeDtypeStruct((2 * halo, grid), BF16),
        in_specs=far,
        out_specs=pl.BlockSpec(memory_space=pltpu.VMEM),
        scratch_shapes=[pltpu.VMEM((16, grid), F32), pltpu.SemaphoreType.DMA((4,))],
        compiler_params=limit,
        name="tail",
    )(image, screen)
    before = lax.ppermute(tail, "slab", ring)

    line = (1, vis_row.shape[0])
    place = pl.BlockSpec(memory_space=pltpu.VMEM)
    pay, image, screen, base, slope_x = pl.pallas_call(
        payload_kernel,
        out_shape=[jax.ShapeDtypeStruct((slabs, width), F32), field, field, field, field],
        in_specs=far + whole(6),
        out_specs=whole(5),
        scratch_shapes=[pltpu.VMEM((width, line[1]), F32), pltpu.SemaphoreType.DMA((2,))],
        compiler_params=limit,
        cost_estimate=pl.CostEstimate(flops=30_000_000, bytes_accessed=200_000, transcendentals=0),
        name="payload",
    )(
        image, screen, vis_row.reshape(line), vis_block.reshape(line), vis_column.reshape(line),
        vis_real.reshape(line), vis_imag.reshape(line), vis_weight.reshape(line),
    )
    framed = rows + 8
    send, slope_y = pl.pallas_call(
        spectrum_kernel,
        out_shape=[
            jax.ShapeDtypeStruct((4 * slabs, width), BF16),
            field,
        ],
        in_specs=whole(8),
        out_specs=whole(2),
        scratch_shapes=[
            pltpu.VMEM((framed, grid), F32),
            pltpu.VMEM((framed, grid), F32),
            pltpu.VMEM((rows, grid), F32),
            pltpu.VMEM((2 * width, 2 * width), BF16),
            pltpu.VMEM((4 * slabs, width), F32),
            pltpu.VMEM((width, width), F32),
        ],
        compiler_params=limit,
        name="spectrum",
    )(screen, image, base, before, pay, row_forward, col_cos, col_sin)

    def exchange(block):
        return lax.all_to_all(
            block.reshape(slabs, 4, width), "slab", split_axis=0, concat_axis=0, tiled=True
        ).reshape(4 * slabs, width)

    scale = 1.0 / grid
    back = pl.pallas_call(
        lambda *refs: visibility_kernel(*refs, slots=slots, scale=scale),
        out_shape=jax.ShapeDtypeStruct((4 * slabs, width), BF16),
        in_specs=whole(7),
        out_specs=place,
        scratch_shapes=[
            pltpu.VMEM((4 * slabs, width), F32),
            pltpu.VMEM((2 * width, slots * width), BF16),
            pltpu.VMEM((2 * width, slots * width), BF16),
        ],
        compiler_params=limit,
        name="visibility",
    )(exchange(send), coarse, coarse_back, inner, inner_back, row_cos, row_sin)
    grad = pl.pallas_call(
        lambda *refs: gradient_kernel(*refs, scale=scale),
        out_shape=jax.ShapeDtypeStruct((rows, grid), F32),
        in_specs=whole(6),
        out_specs=place,
        scratch_shapes=[
            pltpu.VMEM((4 * slabs, width), F32),
            pltpu.VMEM((width, 4 * width), F32),
            pltpu.VMEM((rows, grid), F32),
        ],
        compiler_params=limit,
        name="gradient",
    )(exchange(back), slope_x, slope_y, row_back, col_cos, col_sin)
    return grad.reshape(1, rows, grid)


def solution(mesh):
    in_specs = (
        P(("chain", "vis"), "slab", None),
        P(("chain", "slab"), None),
        P("slab"),
        P("slab", None),
        P("slab"),
        P("slab"),
        P("slab"),
        P("slab"),
    )
    out_specs = P(("chain", "vis"), "slab", None)
    return jax.shard_map(local, mesh=mesh, in_specs=in_specs, out_specs=out_specs, check_vma=False)
```

```python
import math

import jax
import jax.numpy as jnp
import numpy as np
from jax import lax
from jax.experimental import pallas as pl
from jax.experimental.pallas import tpu as pltpu
from jax.sharding import PartitionSpec as P

F32 = jnp.float32
BF16 = jnp.bfloat16
NT = (((1,), (1,)), ((), ()))
NN = (((1,), (0,)), ((), ()))
fields = 8
halo = 4
lead = 2


def angle(first, second, length):
    turn = (np.outer(first, second) % length) * (2.0 * math.pi / length)
    return np.cos(turn), np.sin(turn)


def tables(rows, slabs, owned, grid):
    fine = grid // slabs
    c2, k2, k1 = np.arange(slabs), np.arange(slabs // 2), np.arange(fine)
    shifted = np.arange(rows) - lead
    cos, sin = angle(k2, c2, slabs)
    row_forward = np.block([[cos, sin], [-sin, cos]])
    row_back = np.block([[cos, sin], [-sin, cos]])
    col_turn = angle(k1, c2, grid)
    cos, sin = angle(c2, c2, slabs)
    coarse = np.block([[cos, sin], [-sin, cos]])
    cos, sin = angle(shifted, k1, fine)
    eye = np.eye(owned)
    cos, sin = np.kron(eye, cos), np.kron(eye, sin)
    inner = np.block([[cos, -sin], [sin, cos]])
    row_turn = [np.tile(part, (1, owned)) for part in angle(c2, shifted, grid)]
    low = [row_forward, row_back, coarse, coarse.T, inner, inner.T]
    high = [*col_turn, *row_turn]
    return [jnp.asarray(t, BF16) for t in low], [jnp.asarray(t, F32) for t in high]


def payload_kernel(
    image, screen, row, block, column, real, imag, weight,
    out, image_kept, screen_kept, base, slope_x, wide, done,
):
    moves = [
        pltpu.make_async_copy(source, target, done.at[index])
        for index, (source, target) in enumerate(
            ((image, image_kept), (screen, screen_kept))
        )
    ]
    for move in moves:
        move.start()
    vis_count = row.shape[1]
    slabs = out.shape[0]
    hot = (
        lax.broadcasted_iota(jnp.int32, (slabs, vis_count), 0) == block[...]
    ).astype(F32)
    hot_low = hot.astype(BF16)
    earlier = (
        lax.broadcasted_iota(jnp.int32, (vis_count, vis_count), 0)
        < lax.broadcasted_iota(jnp.int32, (vis_count, vis_count), 1)
    ).astype(F32).astype(BF16)
    before = lax.dot_general(hot_low, earlier, NN, preferred_element_type=F32)
    rank = jnp.sum(before * hot, axis=0, keepdims=True)
    ky = row[...]
    parts = [
        jnp.bitwise_and(ky, slabs - 1).astype(F32),
        (column[...] * (slabs // 8) + ky // slabs).astype(F32),
    ]
    for value in (real, imag, weight):
        whole = value[...]
        lead = whole.astype(BF16).astype(F32)
        parts += [lead, whole - lead]
    which = lax.broadcasted_iota(jnp.int32, (fields, vis_count), 0)
    stack = jnp.zeros((fields, vis_count), F32)
    for index, part in enumerate(parts):
        stack = jnp.where(which == index, part, stack)
    for slot in range(slabs // fields):
        wide[slot * fields : (slot + 1) * fields, :] = jnp.where(
            rank == float(slot), stack, 0.0
        )
    out[...] = lax.dot_general(
        hot_low, wide[...].astype(BF16), NT, preferred_element_type=F32
    )
    for move in moves:
        move.wait()
    own = image_kept[...]
    own_x = slope(own, lane_roll)
    slope_x[...] = own_x
    base[...] = own + slope(screen_kept[...], lane_roll) * own_x


def lane_roll(x, shift):
    return pltpu.roll(x, shift % x.shape[1], 1)


def row_roll(x, shift):
    return pltpu.roll(x, shift % x.shape[0], 0)


def slope(x, roll):
    return (8.0 * (roll(x, -1) - roll(x, 1)) - (roll(x, -2) - roll(x, 2))) * (1.0 / 12.0)


def cosine(index, length):
    return math.cos(2.0 * math.pi * (index % length) / length)


def sine(index, length):
    return math.sin(2.0 * math.pi * (index % length) / length)


def weighted(terms):
    total = None
    for factor, value in terms:
        if abs(factor) < 1e-12:
            continue
        if abs(factor - 1.0) < 1e-12:
            term = value
        elif abs(factor + 1.0) < 1e-12:
            term = -value
        else:
            term = factor * value
        total = term if total is None else total + term
    return total


def tail_kernel(image, screen, tail, kept, done):
    rows, grid = image.shape
    below, span = rows - 8, grid // 2
    moves = []
    for index, source in enumerate((image, screen)):
        for side in range(2):
            columns = slice(side * span, (side + 1) * span)
            moves.append(
                pltpu.make_async_copy(
                    source.at[below:rows, columns],
                    kept.at[index * 8 : (index + 1) * 8, columns],
                    done.at[len(moves)],
                )
            )
            moves[-1].start()
    for move in moves:
        move.wait()
    tail[...] = jnp.concatenate(
        [kept[8 - halo : 8, :], kept[16 - halo : 16, :]], 0
    ).astype(BF16)


def spectrum_kernel(
    screen, image, base, before, pay, table, turn_cos, turn_sin,
    out, slope_y, frame, other, joint, folded, packed, relayed,
):
    rows, grid = image.shape
    fine, width = turn_cos.shape
    framed = frame.shape[0]
    edge = before[...].astype(F32)
    for index, (ref, own) in enumerate(((frame, image), (other, screen))):
        part = edge[index * halo : (index + 1) * halo]
        ref[0:lead, :] = part[halo - lead :]
        ref[lead : lead + rows, :] = own[...]
        ref[lead + rows : framed - lead, :] = jnp.zeros((framed - rows - 2 * lead, grid), F32)
        ref[framed - lead :, :] = part[: halo - lead]
    edge_x = slope(edge, lane_roll)
    edge_base = edge[0:halo] + edge_x[halo:] * edge_x[0:halo]
    joint[0:lead, :] = edge_base[halo - lead :]
    joint[lead:, :] = base[0 : rows - lead, :]
    image_y = slope(frame[...], row_roll)
    slope_y[...] = image_y[0:rows]
    for i in range(fine):
        relayed[i * 8 : (i + 1) * 8, :] = image_y[0:8, i * width : (i + 1) * width]
    joined = joint[...] + (slope(other[...], row_roll) * image_y)[0:rows]
    tiles = [joined[:, i * width : (i + 1) * width] for i in range(fine)]
    half = fine // 2
    even = [tiles[j] + tiles[fine - j] for j in range(1, half)]
    odd = [tiles[j] - tiles[fine - j] for j in range(1, half)]
    for k in range(half + 1):
        part_real = weighted(
            [(1.0, tiles[0]), ((-1.0) ** k, tiles[half])]
            + [(cosine(j * k, fine), even[j - 1]) for j in range(1, half)]
        )
        part_imag = weighted([(-sine(j * k, fine), odd[j - 1]) for j in range(1, half)])
        for index in sorted({k, (fine - k) % fine}):
            sign = 1.0 if index == k else -1.0
            cos = turn_cos[index : index + 1, :]
            sin = turn_sin[index : index + 1, :]
            first, second = part_real * cos, part_real * sin
            if part_imag is None:
                value_real, value_imag = first, -second
            else:
                value_real = first + sign * (part_imag * sin)
                value_imag = sign * (part_imag * cos) - second
            span = slice(index * rows, (index + 1) * rows)
            folded[span, 0:width] = value_real.astype(BF16)
            folded[span, width:] = value_imag.astype(BF16)
    spectrum = lax.dot_general(table[...], folded[...], NT, preferred_element_type=F32)
    deep = width // 2
    for side in range(2):
        for part in range(2):
            packed[pl.ds(side * 4 + part, deep, stride=8), :] = spectrum[
                part * deep : (part + 1) * deep, side * width : (side + 1) * width
            ]
    packed[pl.ds(2, width, stride=4), :] = pay[...]
    packed[pl.ds(3, width, stride=4), :] = jnp.transpose(relayed[...])
    out[...] = packed[...].astype(BF16)


def visibility_kernel(
    arrived, coarse, coarse_back, inner, inner_back, turn_cos, turn_sin,
    out, wide, hot, spread, *, slots, scale,
):
    width = arrived.shape[1]
    wide[...] = arrived[...].astype(F32)
    part_real = wide[pl.ds(0, width, stride=4), :]
    part_imag = wide[pl.ds(1, width, stride=4), :]
    pay = jnp.transpose(wide[pl.ds(2, width, stride=4), :])
    relayed = wide[pl.ds(3, width, stride=4), :]
    stacked = jnp.concatenate([part_real, part_imag], 0).astype(BF16)
    mixed = lax.dot_general(coarse[...], stacked, NN, preferred_element_type=F32)
    cos, sin = turn_cos[...], turn_sin[...]
    left, right = mixed[:width], mixed[width:]
    turned = jnp.concatenate([left * cos + right * sin, right * cos - left * sin], 1)
    cells = scale * jnp.transpose(
        lax.dot_general(turned.astype(BF16), inner[...], NN, preferred_element_type=F32)
    )
    main = cells.astype(BF16)
    rest = (cells - main.astype(F32)).astype(BF16)
    split = jnp.concatenate([main, rest], 1)
    down = lax.broadcasted_iota(jnp.int32, (width, width), 0).astype(F32)
    for slot in range(slots):
        at = slot * fields
        span = slice(slot * width, (slot + 1) * width)
        one = (pay[at : at + 1, :] == down).astype(F32).astype(BF16)
        hot[0:width, span] = one
        hot[width:, span] = one
    picked = lax.dot_general(split, hot[...], NN, preferred_element_type=F32)
    for slot in range(slots):
        at = slot * fields
        span = slice(slot * width, (slot + 1) * width)
        value = [pay[at + i : at + i + 1, :] for i in range(fields)]
        mask = value[1] == down
        weight = value[6] + value[7]
        for part in range(2):
            model = jnp.sum(
                jnp.where(mask, picked[part * width : (part + 1) * width, span], 0.0),
                axis=0,
                keepdims=True,
            )
            error = weight * (model - (value[2 + 2 * part] + value[3 + 2 * part]))
            spread[part * width : (part + 1) * width, span] = jnp.where(
                mask, error, 0.0
            ).astype(BF16)
    sums = lax.dot_general(
        hot[0:width, :], spread[...], NT, preferred_element_type=F32
    )
    mixed = lax.dot_general(
        sums.astype(BF16), inner_back[...], NN, preferred_element_type=F32
    )
    left, right = mixed[:, :width], mixed[:, width:]
    turned = jnp.concatenate([left * cos - right * sin, right * cos + left * sin], 0)
    back = lax.dot_general(
        coarse_back[...], turned.astype(BF16), NN, preferred_element_type=F32
    )
    place = jnp.bitwise_and(lax.broadcasted_iota(jnp.int32, (width, width), 1), 15)
    real, imag = back[:width], back[width:]
    wide[pl.ds(0, width, stride=4), :] = real
    wide[pl.ds(1, width, stride=4), :] = imag
    wide[pl.ds(2, width, stride=4), :] = jnp.where(
        place < 8, row_roll(real, -1), lane_roll(row_roll(imag, -1), 8)
    )
    wide[pl.ds(3, width, stride=4), :] = row_roll(relayed, -1)
    out[...] = wide[...].astype(BF16)


def gradient_kernel(
    arrived, slope_x, slope_y, table, turn_cos, turn_sin,
    out, wide, grouped, result, done, *, scale,
):
    rows, grid = slope_x.shape
    fine, width = turn_cos.shape
    deep = width // 2
    half = fine // 2
    wide[...] = arrived[...].astype(F32)
    next_y = jnp.transpose(wide[pl.ds(3, width, stride=4), :])
    for side in range(2):
        both = wide[pl.ds(side * 4 + 2, deep, stride=8), :]
        for part in range(2):
            down = slice(part * deep, (part + 1) * deep)
            grouped[down, side * width : (side + 1) * width] = wide[
                pl.ds(side * 4 + part, deep, stride=8), :
            ]
            grouped[down, (2 + side) * width : (3 + side) * width] = (
                both if part == 0 else lane_roll(both, -8)
            )
    flat = jnp.transpose(grouped[...]).astype(BF16)
    mixed = lax.dot_general(flat, table[...], NN, preferred_element_type=F32)
    below = fine * rows
    real, imag = [], []
    for k in range(fine):
        cos = scale * turn_cos[k : k + 1, :]
        sin = scale * turn_sin[k : k + 1, :]
        at = k * rows
        both = jnp.concatenate([mixed[at : at + rows], mixed[below + at : below + at + 8]], 0)
        left, right = both[:, 0:width], both[:, width:]
        real.append(left * cos - right * sin)
        imag.append(right * cos + left * sin)
    even = [real[k] + real[fine - k] for k in range(1, half)]
    odd = [imag[k] - imag[fine - k] for k in range(1, half)]
    lane = lax.broadcasted_iota(jnp.int32, (rows, width), 1)
    parts, turned, finished, moves = {}, {}, set(), {}
    for c in range(half + 1):
        plain = weighted(
            [(1.0, real[0]), ((-1.0) ** c, real[half])]
            + [(cosine(c * k, fine), even[k - 1]) for k in range(1, half)]
        )
        cross = weighted([(sine(c * k, fine), odd[k - 1]) for k in range(1, half)])
        for index in sorted({c, (fine - c) % fine}):
            if cross is None:
                value = plain
            else:
                value = plain - cross if index == c else plain + cross
            span = slice(index * width, (index + 1) * width)
            push_x = row_roll(value, -lead)[0:rows] * slope_x[:, span]
            turned[index] = {step: lane_roll(push_x, -step) for step in (-2, -1, 1, 2)}
            push_y = value * jnp.concatenate(
                [slope_y[:, span], next_y[index * 8 : (index + 1) * 8]], 0
            )
            change = 8.0 * (row_roll(push_y, -1) - row_roll(push_y, -3)) - (
                push_y - row_roll(push_y, -4)
            )
            parts[index] = change[0:rows] * (1.0 / 12.0)
        for index in range(fine):
            left, right = (index - 1) % fine, (index + 1) % fine
            if index in finished or not {left, index, right} <= parts.keys():
                continue
            near = {
                step: jnp.where(
                    lane < width - step if step > 0 else lane >= -step,
                    turned[index][step],
                    turned[right if step > 0 else left][step],
                )
                for step in (-2, -1, 1, 2)
            }
            change = 8.0 * (near[1] - near[-1]) - (near[2] - near[-2])
            result[:, index * width : (index + 1) * width] = (
                parts[index] - change * (1.0 / 12.0)
            )
            finished.add(index)
        for pair in range(half):
            if pair in moves or not {2 * pair, 2 * pair + 1} <= finished:
                continue
            span = slice(2 * pair * width, (2 * pair + 2) * width)
            moves[pair] = pltpu.make_async_copy(
                result.at[:, span], out.at[:, span], done.at[pair]
            )
            moves[pair].start()
    for pair in range(half):
        moves[pair].wait()


def whole(count):
    return [pl.BlockSpec(memory_space=pltpu.VMEM)] * count


def local(screens, image, vis_row, vis_block, vis_column, vis_real, vis_imag, vis_weight):
    rows, grid = image.shape
    slabs = lax.axis_size("slab")
    owned = grid // 2 // slabs
    slots = 3 * vis_row.shape[0] // slabs
    screen = screens.reshape(rows, grid)
    low, high = tables(rows, slabs, owned, grid)
    row_forward, row_back, coarse, coarse_back, inner, inner_back = low
    col_cos, col_sin, row_cos, row_sin = high
    width = slabs

    ring = [(i, (i + 1) % slabs) for i in range(slabs)]
    limit = pltpu.CompilerParams(vmem_limit_bytes=12 * 2**20)
    field = jax.ShapeDtypeStruct((rows, grid), F32)
    far = [pl.BlockSpec(memory_space=pltpu.HBM)] * 2
    image, screen = (
        pltpu.with_memory_space_constraint(part, pltpu.HBM) for part in (image, screen)
    )
    tail = pl.pallas_call(
        tail_kernel,
        out_shape=jax.ShapeDtypeStruct((2 * halo, grid), BF16),
        in_specs=far,
        out_specs=pl.BlockSpec(memory_space=pltpu.VMEM),
        scratch_shapes=[pltpu.VMEM((16, grid), F32), pltpu.SemaphoreType.DMA((4,))],
        compiler_params=limit,
        name="tail",
    )(image, screen)
    before = lax.ppermute(tail, "slab", ring)

    line = (1, vis_row.shape[0])
    place = pl.BlockSpec(memory_space=pltpu.VMEM)
    pay, image, screen, base, slope_x = pl.pallas_call(
        payload_kernel,
        out_shape=[jax.ShapeDtypeStruct((slabs, width), F32), field, field, field, field],
        in_specs=far + whole(6),
        out_specs=whole(5),
        scratch_shapes=[pltpu.VMEM((width, line[1]), F32), pltpu.SemaphoreType.DMA((2,))],
        compiler_params=limit,
        cost_estimate=pl.CostEstimate(flops=30_000_000, bytes_accessed=200_000, transcendentals=0),
        name="payload",
    )(
        image, screen, vis_row.reshape(line), vis_block.reshape(line), vis_column.reshape(line),
        vis_real.reshape(line), vis_imag.reshape(line), vis_weight.reshape(line),
    )
    framed = rows + 8
    send, slope_y = pl.pallas_call(
        spectrum_kernel,
        out_shape=[
            jax.ShapeDtypeStruct((4 * slabs, width), BF16),
            field,
        ],
        in_specs=whole(8),
        out_specs=whole(2),
        scratch_shapes=[
            pltpu.VMEM((framed, grid), F32),
            pltpu.VMEM((framed, grid), F32),
            pltpu.VMEM((rows, grid), F32),
            pltpu.VMEM((2 * width, 2 * width), BF16),
            pltpu.VMEM((4 * slabs, width), F32),
            pltpu.VMEM((width, width), F32),
        ],
        compiler_params=limit,
        name="spectrum",
    )(screen, image, base, before, pay, row_forward, col_cos, col_sin)

    def exchange(block):
        return lax.all_to_all(
            block.reshape(slabs, 4, width), "slab", split_axis=0, concat_axis=0, tiled=True
        ).reshape(4 * slabs, width)

    scale = 1.0 / grid
    back = pl.pallas_call(
        lambda *refs: visibility_kernel(*refs, slots=slots, scale=scale),
        out_shape=jax.ShapeDtypeStruct((4 * slabs, width), BF16),
        in_specs=whole(7),
        out_specs=place,
        scratch_shapes=[
            pltpu.VMEM((4 * slabs, width), F32),
            pltpu.VMEM((2 * width, slots * width), BF16),
            pltpu.VMEM((2 * width, slots * width), BF16),
        ],
        compiler_params=limit,
        name="visibility",
    )(exchange(send), coarse, coarse_back, inner, inner_back, row_cos, row_sin)
    grad = pl.pallas_call(
        lambda *refs: gradient_kernel(*refs, scale=scale),
        out_shape=jax.ShapeDtypeStruct((rows, grid), F32),
        in_specs=whole(6),
        out_specs=pl.BlockSpec(memory_space=pltpu.HBM),
        scratch_shapes=[
            pltpu.VMEM((4 * slabs, width), F32),
            pltpu.VMEM((width, 4 * width), F32),
            pltpu.VMEM((rows, grid), F32),
            pltpu.SemaphoreType.DMA((grid // slabs // 2,)),
        ],
        compiler_params=limit,
        name="gradient",
    )(exchange(back), slope_x, slope_y, row_back, col_cos, col_sin)
    return grad.reshape(1, rows, grid)


def solution(mesh):
    in_specs = (
        P(("chain", "vis"), "slab", None),
        P(("chain", "slab"), None),
        P("slab"),
        P("slab", None),
        P("slab"),
        P("slab"),
        P("slab"),
        P("slab"),
    )
    out_specs = P(("chain", "vis"), "slab", None)
    return jax.shard_map(local, mesh=mesh, in_specs=in_specs, out_specs=out_specs, check_vma=False)
```

```python
import math

import jax
import jax.numpy as jnp
import numpy as np
from jax import lax
from jax.experimental import pallas as pl
from jax.experimental.pallas import tpu as pltpu
from jax.sharding import PartitionSpec as P

F32 = jnp.float32
BF16 = jnp.bfloat16
NT = (((1,), (1,)), ((), ()))
NN = (((1,), (0,)), ((), ()))
fields = 8
halo = 4
lead = 2


def angle(first, second, length):
    turn = (np.outer(first, second) % length) * (2.0 * math.pi / length)
    return np.cos(turn), np.sin(turn)


def tables(rows, slabs, owned, grid):
    fine = grid // slabs
    c2, k2, k1 = np.arange(slabs), np.arange(slabs // 2), np.arange(fine)
    shifted = np.arange(rows) - lead
    cos, sin = angle(k2, c2, slabs)
    row_forward = np.block([[cos, sin], [-sin, cos]])
    row_back = np.block([[cos, sin], [-sin, cos]])
    col_turn = angle(k1, c2, grid)
    cos, sin = angle(c2, c2, slabs)
    coarse = np.block([[cos, sin], [-sin, cos]])
    cos, sin = angle(shifted, k1, fine)
    eye = np.eye(owned)
    cos, sin = np.kron(eye, cos), np.kron(eye, sin)
    inner = np.block([[cos, -sin], [sin, cos]])
    row_turn = [np.tile(part, (1, owned)) for part in angle(c2, shifted, grid)]
    low = [row_forward, row_back, coarse, coarse.T, inner.T]
    high = [*col_turn, *row_turn]
    return [jnp.asarray(t, BF16) for t in low], [jnp.asarray(t, F32) for t in high]


def payload_kernel(
    image, screen, row, block, column, real, imag, weight,
    out, image_kept, screen_kept, base, slope_x, wide, done,
):
    moves = [
        pltpu.make_async_copy(source, target, done.at[index])
        for index, (source, target) in enumerate(
            ((image, image_kept), (screen, screen_kept))
        )
    ]
    for move in moves:
        move.start()
    vis_count = row.shape[1]
    slabs = out.shape[0]
    hot = (
        lax.broadcasted_iota(jnp.int32, (slabs, vis_count), 0) == block[...]
    ).astype(F32)
    hot_low = hot.astype(BF16)
    earlier = (
        lax.broadcasted_iota(jnp.int32, (vis_count, vis_count), 0)
        < lax.broadcasted_iota(jnp.int32, (vis_count, vis_count), 1)
    ).astype(F32).astype(BF16)
    before = lax.dot_general(hot_low, earlier, NN, preferred_element_type=F32)
    rank = jnp.sum(before * hot, axis=0, keepdims=True)
    ky = row[...]
    parts = [
        jnp.bitwise_and(ky, slabs - 1).astype(F32),
        (column[...] * (slabs // 8) + ky // slabs).astype(F32),
    ]
    for value in (real, imag, weight):
        whole = value[...]
        lead = whole.astype(BF16).astype(F32)
        parts += [lead, whole - lead]
    which = lax.broadcasted_iota(jnp.int32, (fields, vis_count), 0)
    stack = jnp.zeros((fields, vis_count), F32)
    for index, part in enumerate(parts):
        stack = jnp.where(which == index, part, stack)
    for slot in range(slabs // fields):
        wide[slot * fields : (slot + 1) * fields, :] = jnp.where(
            rank == float(slot), stack, 0.0
        )
    out[...] = lax.dot_general(
        hot_low, wide[...].astype(BF16), NT, preferred_element_type=F32
    )
    for move in moves:
        move.wait()
    own = image_kept[...]
    own_x = slope(own, lane_roll)
    slope_x[...] = own_x
    base[...] = own + slope(screen_kept[...], lane_roll) * own_x


def lane_roll(x, shift):
    return pltpu.roll(x, shift % x.shape[1], 1)


def row_roll(x, shift):
    return pltpu.roll(x, shift % x.shape[0], 0)


def slope(x, roll):
    return (8.0 * (roll(x, -1) - roll(x, 1)) - (roll(x, -2) - roll(x, 2))) * (1.0 / 12.0)


def cosine(index, length):
    return math.cos(2.0 * math.pi * (index % length) / length)


def sine(index, length):
    return math.sin(2.0 * math.pi * (index % length) / length)


def weighted(terms):
    total = None
    for factor, value in terms:
        if abs(factor) < 1e-12:
            continue
        if abs(factor - 1.0) < 1e-12:
            term = value
        elif abs(factor + 1.0) < 1e-12:
            term = -value
        else:
            term = factor * value
        total = term if total is None else total + term
    return total


def tail_kernel(image, screen, tail, kept, done):
    rows, grid = image.shape
    below, span = rows - 8, grid // 2
    moves = []
    for index, source in enumerate((image, screen)):
        for side in range(2):
            columns = slice(side * span, (side + 1) * span)
            moves.append(
                pltpu.make_async_copy(
                    source.at[below:rows, columns],
                    kept.at[index * 8 : (index + 1) * 8, columns],
                    done.at[len(moves)],
                )
            )
            moves[-1].start()
    for move in moves:
        move.wait()
    tail[...] = jnp.concatenate(
        [kept[8 - halo : 8, :], kept[16 - halo : 16, :]], 0
    ).astype(BF16)


def spectrum_kernel(
    screen, image, base, before, pay, table, turn_cos, turn_sin,
    out, slope_y, frame, other, joint, folded, packed, relayed,
):
    rows, grid = image.shape
    fine, width = turn_cos.shape
    framed = frame.shape[0]
    edge = before[...].astype(F32)
    for index, (ref, own) in enumerate(((frame, image), (other, screen))):
        part = edge[index * halo : (index + 1) * halo]
        ref[0:lead, :] = part[halo - lead :]
        ref[lead : lead + rows, :] = own[...]
        ref[lead + rows : framed - lead, :] = jnp.zeros((framed - rows - 2 * lead, grid), F32)
        ref[framed - lead :, :] = part[: halo - lead]
    edge_x = slope(edge, lane_roll)
    edge_base = edge[0:halo] + edge_x[halo:] * edge_x[0:halo]
    joint[0:lead, :] = edge_base[halo - lead :]
    joint[lead:, :] = base[0 : rows - lead, :]
    image_y = slope(frame[...], row_roll)
    slope_y[...] = image_y[0:rows]
    for i in range(fine):
        relayed[i * 8 : (i + 1) * 8, :] = image_y[0:8, i * width : (i + 1) * width]
    joined = joint[...] + (slope(other[...], row_roll) * image_y)[0:rows]
    tiles = [joined[:, i * width : (i + 1) * width] for i in range(fine)]
    half = fine // 2
    even = [tiles[j] + tiles[fine - j] for j in range(1, half)]
    odd = [tiles[j] - tiles[fine - j] for j in range(1, half)]
    for k in range(half + 1):
        part_real = weighted(
            [(1.0, tiles[0]), ((-1.0) ** k, tiles[half])]
            + [(cosine(j * k, fine), even[j - 1]) for j in range(1, half)]
        )
        part_imag = weighted([(-sine(j * k, fine), odd[j - 1]) for j in range(1, half)])
        for index in sorted({k, (fine - k) % fine}):
            sign = 1.0 if index == k else -1.0
            cos = turn_cos[index : index + 1, :]
            sin = turn_sin[index : index + 1, :]
            first, second = part_real * cos, part_real * sin
            if part_imag is None:
                value_real, value_imag = first, -second
            else:
                value_real = first + sign * (part_imag * sin)
                value_imag = sign * (part_imag * cos) - second
            span = slice(index * rows, (index + 1) * rows)
            folded[span, 0:width] = value_real.astype(BF16)
            folded[span, width:] = value_imag.astype(BF16)
    spectrum = lax.dot_general(table[...], folded[...], NT, preferred_element_type=F32)
    deep = width // 2
    for side in range(2):
        for part in range(2):
            packed[pl.ds(side * 4 + part, deep, stride=8), :] = spectrum[
                part * deep : (part + 1) * deep, side * width : (side + 1) * width
            ]
    packed[pl.ds(2, width, stride=4), :] = pay[...]
    packed[pl.ds(3, width, stride=4), :] = jnp.transpose(relayed[...])
    out[...] = packed[...].astype(BF16)


def visibility_kernel(
    arrived, coarse, coarse_back, inner_back, turn_cos, turn_sin,
    out, wide, hot, spread, *, slots, scale,
):
    width = arrived.shape[1]
    wide[...] = arrived[...].astype(F32)
    part_real = wide[pl.ds(0, width, stride=4), :]
    part_imag = wide[pl.ds(1, width, stride=4), :]
    pay = jnp.transpose(wide[pl.ds(2, width, stride=4), :])
    relayed = wide[pl.ds(3, width, stride=4), :]
    stacked = jnp.concatenate([part_real, part_imag], 0).astype(BF16)
    mixed = lax.dot_general(coarse[...], stacked, NN, preferred_element_type=F32)
    cos, sin = turn_cos[...], turn_sin[...]
    left, right = mixed[:width], mixed[width:]
    turned = jnp.concatenate([left * cos + right * sin, right * cos - left * sin], 1)
    cells = scale * lax.dot_general(
        inner_back[...], turned.astype(BF16), NT, preferred_element_type=F32
    )
    main = cells.astype(BF16)
    rest = (cells - main.astype(F32)).astype(BF16)
    split = jnp.concatenate([main, rest], 1)
    down = lax.broadcasted_iota(jnp.int32, (width, width), 0).astype(F32)
    for slot in range(slots):
        at = slot * fields
        span = slice(slot * width, (slot + 1) * width)
        one = (pay[at : at + 1, :] == down).astype(F32).astype(BF16)
        hot[0:width, span] = one
        hot[width:, span] = one
    picked = lax.dot_general(split, hot[...], NN, preferred_element_type=F32)
    for slot in range(slots):
        at = slot * fields
        span = slice(slot * width, (slot + 1) * width)
        value = [pay[at + i : at + i + 1, :] for i in range(fields)]
        mask = value[1] == down
        weight = value[6] + value[7]
        for part in range(2):
            model = jnp.sum(
                jnp.where(mask, picked[part * width : (part + 1) * width, span], 0.0),
                axis=0,
                keepdims=True,
            )
            error = weight * (model - (value[2 + 2 * part] + value[3 + 2 * part]))
            spread[part * width : (part + 1) * width, span] = jnp.where(
                mask, error, 0.0
            ).astype(BF16)
    sums = lax.dot_general(
        hot[0:width, :], spread[...], NT, preferred_element_type=F32
    )
    mixed = lax.dot_general(
        sums.astype(BF16), inner_back[...], NN, preferred_element_type=F32
    )
    left, right = mixed[:, :width], mixed[:, width:]
    turned = jnp.concatenate([left * cos - right * sin, right * cos + left * sin], 0)
    back = lax.dot_general(
        coarse_back[...], turned.astype(BF16), NN, preferred_element_type=F32
    )
    place = jnp.bitwise_and(lax.broadcasted_iota(jnp.int32, (width, width), 1), 15)
    real, imag = back[:width], back[width:]
    wide[pl.ds(0, width, stride=4), :] = real
    wide[pl.ds(1, width, stride=4), :] = imag
    wide[pl.ds(2, width, stride=4), :] = jnp.where(
        place < 8, row_roll(real, -1), lane_roll(row_roll(imag, -1), 8)
    )
    wide[pl.ds(3, width, stride=4), :] = row_roll(relayed, -1)
    out[...] = wide[...].astype(BF16)


def gradient_kernel(
    arrived, slope_x, slope_y, table, turn_cos, turn_sin,
    out, wide, grouped, push_x, *, scale,
):
    rows, grid = slope_x.shape
    fine, width = turn_cos.shape
    deep = width // 2
    half = fine // 2
    wide[...] = arrived[...].astype(F32)
    next_y = jnp.transpose(wide[pl.ds(3, width, stride=4), :])
    for side in range(2):
        both = wide[pl.ds(side * 4 + 2, deep, stride=8), :]
        for part in range(2):
            down = slice(part * deep, (part + 1) * deep)
            grouped[down, side * width : (side + 1) * width] = wide[
                pl.ds(side * 4 + part, deep, stride=8), :
            ]
            grouped[down, (2 + side) * width : (3 + side) * width] = (
                both if part == 0 else lane_roll(both, -8)
            )
    flat = jnp.transpose(grouped[...].astype(BF16))
    mixed = lax.dot_general(flat, table[...], NN, preferred_element_type=F32)
    below = fine * rows
    real, imag = [], []
    for k in range(fine):
        cos = scale * turn_cos[k : k + 1, :]
        sin = scale * turn_sin[k : k + 1, :]
        at = k * rows
        both = jnp.concatenate([mixed[at : at + rows], mixed[below + at : below + at + 8]], 0)
        left, right = both[:, 0:width], both[:, width:]
        real.append(left * cos - right * sin)
        imag.append(right * cos + left * sin)
    even = [real[k] + real[fine - k] for k in range(1, half)]
    odd = [imag[k] - imag[fine - k] for k in range(1, half)]
    for c in range(half + 1):
        plain = weighted(
            [(1.0, real[0]), ((-1.0) ** c, real[half])]
            + [(cosine(c * k, fine), even[k - 1]) for k in range(1, half)]
        )
        cross = weighted([(sine(c * k, fine), odd[k - 1]) for k in range(1, half)])
        for index in sorted({c, (fine - c) % fine}):
            if cross is None:
                value = plain
            else:
                value = plain - cross if index == c else plain + cross
            span = slice(index * width, (index + 1) * width)
            push_x[:, span] = row_roll(value, -lead)[0:rows] * slope_x[:, span]
            push_y = value * jnp.concatenate(
                [slope_y[:, span], next_y[index * 8 : (index + 1) * 8]], 0
            )
            change = 8.0 * (row_roll(push_y, -1) - row_roll(push_y, -3)) - (
                push_y - row_roll(push_y, -4)
            )
            out[:, span] = change[0:rows] * (1.0 / 12.0)
    out[...] = out[...] - slope(push_x[...], lane_roll)


def whole(count):
    return [pl.BlockSpec(memory_space=pltpu.VMEM)] * count


def local(screens, image, vis_row, vis_block, vis_column, vis_real, vis_imag, vis_weight):
    rows, grid = image.shape
    slabs = lax.axis_size("slab")
    owned = grid // 2 // slabs
    slots = 3 * vis_row.shape[0] // slabs
    screen = screens.reshape(rows, grid)
    low, high = tables(rows, slabs, owned, grid)
    row_forward, row_back, coarse, coarse_back, inner_back = low
    col_cos, col_sin, row_cos, row_sin = high
    width = slabs

    ring = [(i, (i + 1) % slabs) for i in range(slabs)]
    limit = pltpu.CompilerParams(vmem_limit_bytes=12 * 2**20)
    field = jax.ShapeDtypeStruct((rows, grid), F32)
    far = [pl.BlockSpec(memory_space=pltpu.HBM)] * 2
    image, screen = (
        pltpu.with_memory_space_constraint(part, pltpu.HBM) for part in (image, screen)
    )
    tail = pl.pallas_call(
        tail_kernel,
        out_shape=jax.ShapeDtypeStruct((2 * halo, grid), BF16),
        in_specs=far,
        out_specs=pl.BlockSpec(memory_space=pltpu.VMEM),
        scratch_shapes=[pltpu.VMEM((16, grid), F32), pltpu.SemaphoreType.DMA((4,))],
        compiler_params=limit,
        name="tail",
    )(image, screen)
    before = lax.ppermute(tail, "slab", ring)

    line = (1, vis_row.shape[0])
    place = pl.BlockSpec(memory_space=pltpu.VMEM)
    pay, image, screen, base, slope_x = pl.pallas_call(
        payload_kernel,
        out_shape=[jax.ShapeDtypeStruct((slabs, width), F32), field, field, field, field],
        in_specs=far + whole(6),
        out_specs=whole(5),
        scratch_shapes=[pltpu.VMEM((width, line[1]), F32), pltpu.SemaphoreType.DMA((2,))],
        compiler_params=limit,
        cost_estimate=pl.CostEstimate(flops=30_000_000, bytes_accessed=200_000, transcendentals=0),
        name="payload",
    )(
        image, screen, vis_row.reshape(line), vis_block.reshape(line), vis_column.reshape(line),
        vis_real.reshape(line), vis_imag.reshape(line), vis_weight.reshape(line),
    )
    framed = rows + 8
    send, slope_y = pl.pallas_call(
        spectrum_kernel,
        out_shape=[
            jax.ShapeDtypeStruct((4 * slabs, width), BF16),
            field,
        ],
        in_specs=whole(8),
        out_specs=whole(2),
        scratch_shapes=[
            pltpu.VMEM((framed, grid), F32),
            pltpu.VMEM((framed, grid), F32),
            pltpu.VMEM((rows, grid), F32),
            pltpu.VMEM((2 * width, 2 * width), BF16),
            pltpu.VMEM((4 * slabs, width), F32),
            pltpu.VMEM((width, width), F32),
        ],
        compiler_params=limit,
        name="spectrum",
    )(screen, image, base, before, pay, row_forward, col_cos, col_sin)

    def exchange(block):
        return lax.all_to_all(
            block.reshape(slabs, 4, width), "slab", split_axis=0, concat_axis=0, tiled=True
        ).reshape(4 * slabs, width)

    scale = 1.0 / grid
    back = pl.pallas_call(
        lambda *refs: visibility_kernel(*refs, slots=slots, scale=scale),
        out_shape=jax.ShapeDtypeStruct((4 * slabs, width), BF16),
        in_specs=whole(6),
        out_specs=place,
        scratch_shapes=[
            pltpu.VMEM((4 * slabs, width), F32),
            pltpu.VMEM((2 * width, slots * width), BF16),
            pltpu.VMEM((2 * width, slots * width), BF16),
        ],
        compiler_params=limit,
        name="visibility",
    )(exchange(send), coarse, coarse_back, inner_back, row_cos, row_sin)
    grad = pl.pallas_call(
        lambda *refs: gradient_kernel(*refs, scale=scale),
        out_shape=jax.ShapeDtypeStruct((rows, grid), F32),
        in_specs=whole(6),
        out_specs=place,
        scratch_shapes=[
            pltpu.VMEM((4 * slabs, width), F32),
            pltpu.VMEM((width, 4 * width), F32),
            pltpu.VMEM((rows, grid), F32),
        ],
        compiler_params=limit,
        name="gradient",
    )(exchange(back), slope_x, slope_y, row_back, col_cos, col_sin)
    return grad.reshape(1, rows, grid)


def solution(mesh):
    in_specs = (
        P(("chain", "vis"), "slab", None),
        P(("chain", "slab"), None),
        P("slab"),
        P("slab", None),
        P("slab"),
        P("slab"),
        P("slab"),
        P("slab"),
    )
    out_specs = P(("chain", "vis"), "slab", None)
    return jax.shard_map(local, mesh=mesh, in_specs=in_specs, out_specs=out_specs, check_vma=False)
```

```python
import math

import jax
import jax.numpy as jnp
import numpy as np
from jax import lax
from jax.experimental import pallas as pl
from jax.experimental.pallas import tpu as pltpu
from jax.sharding import PartitionSpec as P

F32 = jnp.float32
BF16 = jnp.bfloat16
NT = (((1,), (1,)), ((), ()))
NN = (((1,), (0,)), ((), ()))
fields = 8
halo = 4
lead = 2


def angle(first, second, length):
    turn = (np.outer(first, second) % length) * (2.0 * math.pi / length)
    return np.cos(turn), np.sin(turn)


def tables(rows, slabs, owned, grid):
    fine = grid // slabs
    c2, k2, k1 = np.arange(slabs), np.arange(slabs // 2), np.arange(fine)
    shifted = np.arange(rows) - lead
    cos, sin = angle(k2, c2, slabs)
    row_forward = np.block([[cos, sin], [-sin, cos]])
    row_back = np.block([[cos, sin], [-sin, cos]])
    col_turn = angle(k1, c2, grid)
    cos, sin = angle(c2, c2, slabs)
    coarse = np.block([[cos, sin], [-sin, cos]])
    cos, sin = angle(shifted, k1, fine)
    eye = np.eye(owned)
    cos, sin = np.kron(eye, cos), np.kron(eye, sin)
    inner = np.block([[cos, -sin], [sin, cos]])
    row_turn = [np.tile(part, (1, owned)) for part in angle(c2, shifted, grid)]
    low = [row_forward, row_back, coarse, coarse.T, inner.T]
    high = [*col_turn, *row_turn]
    return [jnp.asarray(t, BF16) for t in low], [jnp.asarray(t, F32) for t in high]


def payload_kernel(
    image, screen, row, block, column, real, imag, weight,
    out, image_kept, screen_kept, base, slope_x, wide, done,
):
    moves = [
        pltpu.make_async_copy(source, target, done.at[index])
        for index, (source, target) in enumerate(
            ((image, image_kept), (screen, screen_kept))
        )
    ]
    for move in moves:
        move.start()
    vis_count = row.shape[1]
    slabs = out.shape[0]
    hot = (
        lax.broadcasted_iota(jnp.int32, (slabs, vis_count), 0) == block[...]
    ).astype(F32)
    hot_low = hot.astype(BF16)
    earlier = (
        lax.broadcasted_iota(jnp.int32, (vis_count, vis_count), 0)
        < lax.broadcasted_iota(jnp.int32, (vis_count, vis_count), 1)
    ).astype(F32).astype(BF16)
    before = lax.dot_general(hot_low, earlier, NN, preferred_element_type=F32)
    rank = jnp.sum(before * hot, axis=0, keepdims=True)
    ky = row[...]
    parts = [
        jnp.bitwise_and(ky, slabs - 1).astype(F32),
        (column[...] * (slabs // 8) + ky // slabs).astype(F32),
    ]
    for value in (real, imag, weight):
        whole = value[...]
        lead = whole.astype(BF16).astype(F32)
        parts += [lead, whole - lead]
    which = lax.broadcasted_iota(jnp.int32, (fields, vis_count), 0)
    stack = jnp.zeros((fields, vis_count), F32)
    for index, part in enumerate(parts):
        stack = jnp.where(which == index, part, stack)
    for slot in range(slabs // fields):
        wide[slot * fields : (slot + 1) * fields, :] = jnp.where(
            rank == float(slot), stack, 0.0
        )
    out[...] = lax.dot_general(
        hot_low, wide[...].astype(BF16), NT, preferred_element_type=F32
    )
    for move in moves:
        move.wait()
    own = image_kept[...]
    own_x = slope(own, lane_roll)
    slope_x[...] = own_x
    base[...] = own + slope(screen_kept[...], lane_roll) * own_x


def lane_roll(x, shift):
    return pltpu.roll(x, shift % x.shape[1], 1)


def row_roll(x, shift):
    return pltpu.roll(x, shift % x.shape[0], 0)


def slope(x, roll):
    return (8.0 * (roll(x, -1) - roll(x, 1)) - (roll(x, -2) - roll(x, 2))) * (1.0 / 12.0)


def cosine(index, length):
    return math.cos(2.0 * math.pi * (index % length) / length)


def sine(index, length):
    return math.sin(2.0 * math.pi * (index % length) / length)


def weighted(terms):
    total = None
    for factor, value in terms:
        if abs(factor) < 1e-12:
            continue
        if abs(factor - 1.0) < 1e-12:
            term = value
        elif abs(factor + 1.0) < 1e-12:
            term = -value
        else:
            term = factor * value
        total = term if total is None else total + term
    return total


def tail_kernel(image, screen, tail, kept, done):
    rows, grid = image.shape
    below, span = rows - 8, grid // 2
    moves = []
    for index, source in enumerate((image, screen)):
        for side in range(2):
            columns = slice(side * span, (side + 1) * span)
            moves.append(
                pltpu.make_async_copy(
                    source.at[below:rows, columns],
                    kept.at[index * 8 : (index + 1) * 8, columns],
                    done.at[len(moves)],
                )
            )
            moves[-1].start()
    for move in moves:
        move.wait()
    tail[...] = jnp.concatenate(
        [kept[8 - halo : 8, :], kept[16 - halo : 16, :]], 0
    ).astype(BF16)


def spectrum_kernel(
    screen, image, base, before, pay, table, turn_cos, turn_sin,
    out, slope_y, frame, other, joint, folded, packed, relayed,
):
    rows, grid = image.shape
    fine, width = turn_cos.shape
    framed = frame.shape[0]
    edge = before[...].astype(F32)
    for index, (ref, own) in enumerate(((frame, image), (other, screen))):
        part = edge[index * halo : (index + 1) * halo]
        ref[0:lead, :] = part[halo - lead :]
        ref[lead : lead + rows, :] = own[...]
        ref[lead + rows : framed - lead, :] = jnp.zeros((framed - rows - 2 * lead, grid), F32)
        ref[framed - lead :, :] = part[: halo - lead]
    edge_x = slope(edge, lane_roll)
    edge_base = edge[0:halo] + edge_x[halo:] * edge_x[0:halo]
    joint[0:lead, :] = edge_base[halo - lead :]
    joint[lead:, :] = base[0 : rows - lead, :]
    image_y = slope(frame[...], row_roll)
    slope_y[...] = image_y[0:rows]
    for i in range(fine):
        relayed[i * 8 : (i + 1) * 8, :] = image_y[0:8, i * width : (i + 1) * width]
    joined = joint[...] + (slope(other[...], row_roll) * image_y)[0:rows]
    tiles = [joined[:, i * width : (i + 1) * width] for i in range(fine)]
    half = fine // 2
    even = [tiles[j] + tiles[fine - j] for j in range(1, half)]
    odd = [tiles[j] - tiles[fine - j] for j in range(1, half)]
    for k in range(half + 1):
        part_real = weighted(
            [(1.0, tiles[0]), ((-1.0) ** k, tiles[half])]
            + [(cosine(j * k, fine), even[j - 1]) for j in range(1, half)]
        )
        part_imag = weighted([(-sine(j * k, fine), odd[j - 1]) for j in range(1, half)])
        for index in sorted({k, (fine - k) % fine}):
            sign = 1.0 if index == k else -1.0
            cos = turn_cos[index : index + 1, :]
            sin = turn_sin[index : index + 1, :]
            first, second = part_real * cos, part_real * sin
            if part_imag is None:
                value_real, value_imag = first, -second
            else:
                value_real = first + sign * (part_imag * sin)
                value_imag = sign * (part_imag * cos) - second
            span = slice(index * rows, (index + 1) * rows)
            folded[span, 0:width] = value_real.astype(BF16)
            folded[span, width:] = value_imag.astype(BF16)
    spectrum = lax.dot_general(table[...], folded[...], NT, preferred_element_type=F32)
    deep = width // 2
    for side in range(2):
        for part in range(2):
            packed[pl.ds(side * 4 + part, deep, stride=8), :] = spectrum[
                part * deep : (part + 1) * deep, side * width : (side + 1) * width
            ]
    packed[pl.ds(2, width, stride=4), :] = pay[...]
    packed[pl.ds(3, width, stride=4), :] = jnp.transpose(relayed[...].astype(BF16)).astype(F32)
    out[...] = packed[...].astype(BF16)


def visibility_kernel(
    arrived, coarse, coarse_back, inner_back, turn_cos, turn_sin,
    out, wide, hot, spread, *, slots, scale,
):
    width = arrived.shape[1]
    wide[...] = arrived[...].astype(F32)
    part_real = wide[pl.ds(0, width, stride=4), :]
    part_imag = wide[pl.ds(1, width, stride=4), :]
    pay = jnp.transpose(wide[pl.ds(2, width, stride=4), :].astype(BF16)).astype(F32)
    relayed = wide[pl.ds(3, width, stride=4), :]
    stacked = jnp.concatenate([part_real, part_imag], 0).astype(BF16)
    mixed = lax.dot_general(coarse[...], stacked, NN, preferred_element_type=F32)
    cos, sin = turn_cos[...], turn_sin[...]
    left, right = mixed[:width], mixed[width:]
    turned = jnp.concatenate([left * cos + right * sin, right * cos - left * sin], 1)
    cells = scale * lax.dot_general(
        inner_back[...], turned.astype(BF16), NT, preferred_element_type=F32
    )
    main = cells.astype(BF16)
    rest = (cells - main.astype(F32)).astype(BF16)
    split = jnp.concatenate([main, rest], 1)
    down = lax.broadcasted_iota(jnp.int32, (width, width), 0).astype(F32)
    for slot in range(slots):
        at = slot * fields
        span = slice(slot * width, (slot + 1) * width)
        one = (pay[at : at + 1, :] == down).astype(F32).astype(BF16)
        hot[0:width, span] = one
        hot[width:, span] = one
    picked = lax.dot_general(split, hot[...], NN, preferred_element_type=F32)
    for slot in range(slots):
        at = slot * fields
        span = slice(slot * width, (slot + 1) * width)
        value = [pay[at + i : at + i + 1, :] for i in range(fields)]
        mask = value[1] == down
        weight = value[6] + value[7]
        for part in range(2):
            model = jnp.sum(
                jnp.where(mask, picked[part * width : (part + 1) * width, span], 0.0),
                axis=0,
                keepdims=True,
            )
            error = weight * (model - (value[2 + 2 * part] + value[3 + 2 * part]))
            spread[part * width : (part + 1) * width, span] = jnp.where(
                mask, error, 0.0
            ).astype(BF16)
    sums = lax.dot_general(
        hot[0:width, :], spread[...], NT, preferred_element_type=F32
    )
    mixed = lax.dot_general(
        sums.astype(BF16), inner_back[...], NN, preferred_element_type=F32
    )
    left, right = mixed[:, :width], mixed[:, width:]
    turned = jnp.concatenate([left * cos - right * sin, right * cos + left * sin], 0)
    back = lax.dot_general(
        coarse_back[...], turned.astype(BF16), NN, preferred_element_type=F32
    )
    place = jnp.bitwise_and(lax.broadcasted_iota(jnp.int32, (width, width), 1), 15)
    real, imag = back[:width], back[width:]
    wide[pl.ds(0, width, stride=4), :] = real
    wide[pl.ds(1, width, stride=4), :] = imag
    wide[pl.ds(2, width, stride=4), :] = jnp.where(
        place < 8, row_roll(real, -1), lane_roll(row_roll(imag, -1), 8)
    )
    wide[pl.ds(3, width, stride=4), :] = row_roll(relayed, -1)
    out[...] = wide[...].astype(BF16)


def gradient_kernel(
    arrived, slope_x, slope_y, table, turn_cos, turn_sin,
    out, wide, grouped, push_x, *, scale,
):
    rows, grid = slope_x.shape
    fine, width = turn_cos.shape
    deep = width // 2
    half = fine // 2
    wide[...] = arrived[...].astype(F32)
    next_y = jnp.transpose(wide[pl.ds(3, width, stride=4), :].astype(BF16)).astype(F32)
    for side in range(2):
        both = wide[pl.ds(side * 4 + 2, deep, stride=8), :]
        for part in range(2):
            down = slice(part * deep, (part + 1) * deep)
            grouped[down, side * width : (side + 1) * width] = wide[
                pl.ds(side * 4 + part, deep, stride=8), :
            ]
            grouped[down, (2 + side) * width : (3 + side) * width] = (
                both if part == 0 else lane_roll(both, -8)
            )
    flat = jnp.transpose(grouped[...].astype(BF16))
    mixed = lax.dot_general(flat, table[...], NN, preferred_element_type=F32)
    below = fine * rows
    real, imag = [], []
    for k in range(fine):
        cos = scale * turn_cos[k : k + 1, :]
        sin = scale * turn_sin[k : k + 1, :]
        at = k * rows
        both = jnp.concatenate([mixed[at : at + rows], mixed[below + at : below + at + 8]], 0)
        left, right = both[:, 0:width], both[:, width:]
        real.append(left * cos - right * sin)
        imag.append(right * cos + left * sin)
    even = [real[k] + real[fine - k] for k in range(1, half)]
    odd = [imag[k] - imag[fine - k] for k in range(1, half)]
    for c in range(half + 1):
        plain = weighted(
            [(1.0, real[0]), ((-1.0) ** c, real[half])]
            + [(cosine(c * k, fine), even[k - 1]) for k in range(1, half)]
        )
        cross = weighted([(sine(c * k, fine), odd[k - 1]) for k in range(1, half)])
        for index in sorted({c, (fine - c) % fine}):
            if cross is None:
                value = plain
            else:
                value = plain - cross if index == c else plain + cross
            span = slice(index * width, (index + 1) * width)
            push_x[:, span] = row_roll(value, -lead)[0:rows] * slope_x[:, span]
            push_y = value * jnp.concatenate(
                [slope_y[:, span], next_y[index * 8 : (index + 1) * 8]], 0
            )
            change = 8.0 * (row_roll(push_y, -1) - row_roll(push_y, -3)) - (
                push_y - row_roll(push_y, -4)
            )
            out[:, span] = change[0:rows] * (1.0 / 12.0)
    out[...] = out[...] - slope(push_x[...], lane_roll)


def whole(count):
    return [pl.BlockSpec(memory_space=pltpu.VMEM)] * count


def local(screens, image, vis_row, vis_block, vis_column, vis_real, vis_imag, vis_weight):
    rows, grid = image.shape
    slabs = lax.axis_size("slab")
    owned = grid // 2 // slabs
    slots = 3 * vis_row.shape[0] // slabs
    screen = screens.reshape(rows, grid)
    low, high = tables(rows, slabs, owned, grid)
    row_forward, row_back, coarse, coarse_back, inner_back = low
    col_cos, col_sin, row_cos, row_sin = high
    width = slabs

    ring = [(i, (i + 1) % slabs) for i in range(slabs)]
    limit = pltpu.CompilerParams(vmem_limit_bytes=12 * 2**20)
    field = jax.ShapeDtypeStruct((rows, grid), F32)
    far = [pl.BlockSpec(memory_space=pltpu.HBM)] * 2
    image, screen = (
        pltpu.with_memory_space_constraint(part, pltpu.HBM) for part in (image, screen)
    )
    tail = pl.pallas_call(
        tail_kernel,
        out_shape=jax.ShapeDtypeStruct((2 * halo, grid), BF16),
        in_specs=far,
        out_specs=pl.BlockSpec(memory_space=pltpu.VMEM),
        scratch_shapes=[pltpu.VMEM((16, grid), F32), pltpu.SemaphoreType.DMA((4,))],
        compiler_params=limit,
        name="tail",
    )(image, screen)
    before = lax.ppermute(tail, "slab", ring)

    line = (1, vis_row.shape[0])
    place = pl.BlockSpec(memory_space=pltpu.VMEM)
    pay, image, screen, base, slope_x = pl.pallas_call(
        payload_kernel,
        out_shape=[jax.ShapeDtypeStruct((slabs, width), F32), field, field, field, field],
        in_specs=far + whole(6),
        out_specs=whole(5),
        scratch_shapes=[pltpu.VMEM((width, line[1]), F32), pltpu.SemaphoreType.DMA((2,))],
        compiler_params=limit,
        cost_estimate=pl.CostEstimate(flops=30_000_000, bytes_accessed=200_000, transcendentals=0),
        name="payload",
    )(
        image, screen, vis_row.reshape(line), vis_block.reshape(line), vis_column.reshape(line),
        vis_real.reshape(line), vis_imag.reshape(line), vis_weight.reshape(line),
    )
    framed = rows + 8
    send, slope_y = pl.pallas_call(
        spectrum_kernel,
        out_shape=[
            jax.ShapeDtypeStruct((4 * slabs, width), BF16),
            field,
        ],
        in_specs=whole(8),
        out_specs=whole(2),
        scratch_shapes=[
            pltpu.VMEM((framed, grid), F32),
            pltpu.VMEM((framed, grid), F32),
            pltpu.VMEM((rows, grid), F32),
            pltpu.VMEM((2 * width, 2 * width), BF16),
            pltpu.VMEM((4 * slabs, width), F32),
            pltpu.VMEM((width, width), F32),
        ],
        compiler_params=limit,
        name="spectrum",
    )(screen, image, base, before, pay, row_forward, col_cos, col_sin)

    def exchange(block):
        return lax.all_to_all(
            block.reshape(slabs, 4, width), "slab", split_axis=0, concat_axis=0, tiled=True
        ).reshape(4 * slabs, width)

    scale = 1.0 / grid
    back = pl.pallas_call(
        lambda *refs: visibility_kernel(*refs, slots=slots, scale=scale),
        out_shape=jax.ShapeDtypeStruct((4 * slabs, width), BF16),
        in_specs=whole(6),
        out_specs=place,
        scratch_shapes=[
            pltpu.VMEM((4 * slabs, width), F32),
            pltpu.VMEM((2 * width, slots * width), BF16),
            pltpu.VMEM((2 * width, slots * width), BF16),
        ],
        compiler_params=limit,
        name="visibility",
    )(exchange(send), coarse, coarse_back, inner_back, row_cos, row_sin)
    grad = pl.pallas_call(
        lambda *refs: gradient_kernel(*refs, scale=scale),
        out_shape=jax.ShapeDtypeStruct((rows, grid), F32),
        in_specs=whole(6),
        out_specs=place,
        scratch_shapes=[
            pltpu.VMEM((4 * slabs, width), F32),
            pltpu.VMEM((width, 4 * width), F32),
            pltpu.VMEM((rows, grid), F32),
        ],
        compiler_params=limit,
        name="gradient",
    )(exchange(back), slope_x, slope_y, row_back, col_cos, col_sin)
    return grad.reshape(1, rows, grid)


def solution(mesh):
    in_specs = (
        P(("chain", "vis"), "slab", None),
        P(("chain", "slab"), None),
        P("slab"),
        P("slab", None),
        P("slab"),
        P("slab"),
        P("slab"),
        P("slab"),
    )
    out_specs = P(("chain", "vis"), "slab", None)
    return jax.shard_map(local, mesh=mesh, in_specs=in_specs, out_specs=out_specs, check_vma=False)
```
